1024 devices in a mesh: wave: 16 (over y, core), sect: 64 (over x, z).
Axes of the slice: x: 4, y: 8, z: 16, core: 2. Of those that a mesh axis runs over, the one named last changes fastest.
Arguments:
- spec_in: bfloat16 [32, 2, 64, 640], P('wave', None, 'sect'), may hold values from -6 to 6
- pair_low: int32 [32], replicated, may hold values from 1 to 319, as said below
- row_points: int32 [640], replicated, may hold values from 20 to 2576, as said below
- legendre: bfloat16 [32, 640, 640], P('wave'), as said below
- gauss_weight: float32 [640], replicated, may hold values from 0 to 1, as said below
- couple: bfloat16 [64, 64], replicated, may hold values from -0.75 to 0.75
- point_factor: float32 [2, 64, 26240], P(None, 'sect', 'wave'), may hold values from 0.25 to 4
Outputs:
- grid_field: bfloat16 [2, 64, 64, 26240], P(None, None, 'sect', 'wave')
- spec_out: float32 [32, 2, 64, 640], P('wave', None, 'sect')
The draws below stay inside these ranges and needn't reach their ends.
Inputs may be any that keep to these rules, and one draw needn't show every extreme that they name: `pair_low`: the lower wavenumbers are distinct; 1 and 319 are always among them, the others are drawn. row_points[j] = 20 + 4 i where i (0 to 639, counted from the pole) is the row pair at position j; every row pair appears once; the block of 40 positions of one band holds row pairs from every latitude. legendre[p, s, j] is the associated Legendre function of slot s of pair p (slot_wave), normalized to unit integral of its square over -1 to 1, at the northern latitude of the row pair at position j; the southern row has the parity sign. `gauss_weight`: the quadrature weight of the latitude of the row pair at position j, the same for its northern and southern row.
All inputs are finite; a program needn't handle non-finite values.
Results may differ from the reference program's by a relative error of at most 0.0062.
Values may be sent and summed in bfloat16 or wider, within the bound.
No kernel may reach another device: no remote copies, remote signals or barrier semaphores. Data moves between devices by JAX's collectives and lax.ppermute only.
A program may use at most 32 MiB of HBM per device.

```python
import math
import jax
import jax.numpy as jnp
from jax import lax

NMAX = 640
NROWH = 640
NPAIR = 32
FIELDS = 64
ROWS_DEV = 40
SECW = 41
N_SECT = 64


def window_lows(key):
    base_key = jax.random.fold_in(key, 101)
    others = jax.random.permutation(jax.random.fold_in(base_key, 1), NMAX // 2 - 3).astype(jnp.int32) + 2
    extremes = jnp.array([1, NMAX // 2 - 1], dtype=jnp.int32)
    chosen = jnp.concatenate([extremes, others[:NPAIR - 2]])
    shuffle = jax.random.permutation(jax.random.fold_in(base_key, 2), NPAIR)
    return chosen[shuffle]


def latitude_order(key):
    base_key = jax.random.fold_in(key, 202)
    band_count = NROWH // ROWS_DEV
    row_keys = jax.random.split(base_key, ROWS_DEV)
    shuffles = jax.vmap(lambda subkey: jax.random.permutation(subkey, band_count))(row_keys)
    row_index = band_count * jnp.arange(ROWS_DEV, dtype=jnp.int32)[:, None] + shuffles.astype(jnp.int32)
    return jnp.transpose(row_index).reshape(-1)


def colatitude_rows(key):
    row_index = latitude_order(key).astype(jnp.float32)
    return math.pi * (row_index + 0.75) / (2.0 * NROWH + 0.5)


def draw_pair_low(key, part):
    return window_lows(key)


def draw_row_points(key, part):
    return (20 + 4 * latitude_order(key)).astype(jnp.int32)


def draw_gauss_weight(key, part):
    return math.pi / (2.0 * NROWH + 0.5) * jnp.sin(colatitude_rows(key))


def draw_legendre(key, part):
    low_waves = window_lows(key).astype(jnp.float32)
    high_waves = NMAX - low_waves
    colatitude = colatitude_rows(key)
    cosine = jnp.cos(colatitude)
    log_sine = jnp.log(jnp.sin(colatitude))
    counter = jnp.arange(1, NMAX + 1, dtype=jnp.float32)
    growth = jnp.concatenate([jnp.zeros((1,), jnp.float32), jnp.cumsum(0.5 * jnp.log((2.0 * counter + 1.0) / (2.0 * counter)))])
    orders = jnp.stack([low_waves, high_waves])
    starts = jnp.exp(0.5 * math.log(0.5) + growth[orders.astype(jnp.int32)][:, :, None] + orders[:, :, None] * log_sine[None, None, :])

    def advance(state_pair, degree_shift):
        older_value, recent = state_pair
        degrees = jnp.stack([low_waves + degree_shift, jnp.zeros_like(low_waves) + degree_shift])
        top_term = 4.0 * degrees * degrees - 1.0
        bottom_term = jnp.maximum(degrees * degrees - orders * orders, 1.0)
        prior_degree = degrees - 1.0
        upper_term = jnp.maximum(prior_degree * prior_degree - orders * orders, 0.0)
        lower_term = jnp.maximum(4.0 * prior_degree * prior_degree - 1.0, 1.0)
        first_coef = jnp.sqrt(top_term / bottom_term)[:, :, None]
        second_coef = jnp.sqrt(upper_term / lower_term)[:, :, None]
        stepped = first_coef * (cosine[None, None, :] * recent - second_coef * older_value)
        new_value = jnp.where((degrees == orders)[:, :, None], starts, jnp.where((degrees > orders)[:, :, None], stepped, 0.0))
        return ((recent, new_value), new_value.astype(jnp.bfloat16))
    zero_state = jnp.zeros_like(starts)
    final_state, values = lax.scan(advance, (zero_state, zero_state), jnp.arange(NMAX, dtype=jnp.float32))
    slot_index = jnp.arange(NMAX, dtype=jnp.float32)
    chosen = jnp.where((slot_index[:, None] < high_waves[None, :])[:, :, None], values[:, 0], values[:, 1])
    return jnp.transpose(chosen, (1, 0, 2))


def level_of(stream_key, extent, pieces, low, high):
    level = 1.0
    for axis_at, blocks in pieces:
        steps = jax.random.uniform(jax.random.fold_in(jax.random.fold_in(stream_key, 6), axis_at), (blocks,), jnp.float32, low / len(pieces), high / len(pieces))
        level = level * jnp.repeat(jnp.exp(steps), extent[axis_at] // blocks).reshape((-1,) + (1,) * (len(extent) - 1 - axis_at))
    return level


def centred(rng, extent, width, bound, shards=(), kind=jnp.bfloat16):
    entries = width * jax.random.normal(rng, extent, jnp.float32)
    if shards:
        entries = entries * level_of(rng, extent, shards, -0.22, 0.18)
    return jnp.clip(entries, -bound, bound).astype(kind)


def setup_inputs(seed: int = 0) -> dict:
    keys = jax.random.split(jax.random.key(seed), 8)
    return {
        "spec_in": centred(keys[0], (NPAIR, 2, FIELDS, NMAX), 1.0, 6.0, ((0, 16), (2, 64))),
        "pair_low": draw_pair_low(jax.random.fold_in(keys[7], 71), 0),
        "row_points": draw_row_points(jax.random.fold_in(keys[7], 71), 0),
        "legendre": draw_legendre(jax.random.fold_in(keys[7], 71), 0),
        "gauss_weight": draw_gauss_weight(jax.random.fold_in(keys[7], 71), 0),
        "couple": centred(keys[5], (FIELDS, FIELDS), FIELDS ** -0.5, 0.75),
        "point_factor": jnp.clip(jnp.exp(math.log(4.0) - 2.7725887 * jax.random.uniform(keys[6], (2, N_SECT, NROWH * SECW), jnp.float32) ** level_of(keys[6], (2, N_SECT, NROWH * SECW), ((1, 64), (2, 16)), -0.2, 0.2)), 0.25, 4.0),
    }


def slot_tables(pair_low, slot_count):
    slot_index = jnp.arange(slot_count, dtype=jnp.int32)
    lower_wave = pair_low[:, None]
    leading = slot_index[None, :] < slot_count - lower_wave
    order_of = jnp.where(leading, lower_wave, slot_count - lower_wave)
    degree = jnp.where(leading, lower_wave + slot_index[None, :], slot_index[None, :])
    odd_parity = (degree + order_of) % 2 == 1
    return (leading, odd_parity)

def spread_spectral(spec_in, leading, odd_parity):
    parity_sign = jnp.where(odd_parity, -1.0, 1.0).astype(jnp.float32)
    member_mask = jnp.stack([leading, jnp.logical_not(leading)], axis=1).astype(jnp.float32)
    hemisphere = jnp.stack([jnp.ones_like(parity_sign), parity_sign], axis=1)
    slot_factor = (member_mask[:, :, None, :] * hemisphere[:, None, :, :]).astype(jnp.bfloat16)
    return spec_in[:, None, None, :, :, :] * slot_factor[:, :, :, None, None, :]

def block_step(fourier, band_points, factor, wave_list, couple, synth_scale):
    wave_total = wave_list.shape[0]
    block_rows = band_points.shape[0]
    sector_width = (band_points + N_SECT - 1) // N_SECT
    columns = jnp.arange(SECW, dtype=jnp.int32)
    sectors = jnp.arange(N_SECT, dtype=jnp.int32)
    lengths = band_points.astype(jnp.float32)
    inner_index = wave_list[None, None, :] * columns[None, :, None] % band_points[:, None, None]
    inner_angle = 2.0 * math.pi * inner_index.astype(jnp.float32) / lengths[:, None, None]
    trig_table = jnp.concatenate([jnp.cos(inner_angle), -jnp.sin(inner_angle)], axis=2).astype(jnp.bfloat16)
    sector_start = sectors[None, :] * sector_width[:, None]
    outer_index = wave_list[None, None, :] * sector_start[:, :, None] % band_points[:, None, None]
    outer_angle = 2.0 * math.pi * outer_index.astype(jnp.float32) / lengths[:, None, None]
    cos_wide = jnp.cos(outer_angle)[:, None, :, None, :]
    sin_wide = jnp.sin(outer_angle)[:, None, :, None, :]
    valid_mask = (columns[None, None, :] < sector_width[:, None, None]) & (sector_start[:, :, None] + columns[None, None, :] < band_points[:, None, None])
    real_part = jnp.transpose(fourier[:, :, 0].astype(jnp.float32), (3, 1, 2, 0))[:, :, None]
    imag_part = jnp.transpose(fourier[:, :, 1].astype(jnp.float32), (3, 1, 2, 0))[:, :, None]
    rot_cos = synth_scale * (real_part * cos_wide - imag_part * sin_wide)
    rot_sin = synth_scale * (real_part * sin_wide + imag_part * cos_wide)
    rotated = jnp.concatenate([rot_cos, rot_sin], axis=4).astype(jnp.bfloat16)
    grid_tile = jnp.einsum('rhtfq,rcq->rhtfc', rotated.astype(jnp.float32), trig_table.astype(jnp.float32))
    grid_tile = jnp.where(valid_mask[:, None, :, None, :], grid_tile, 0.0).astype(jnp.bfloat16)
    grid_block = jnp.transpose(grid_tile, (1, 3, 2, 0, 4)).reshape(2, FIELDS, N_SECT, block_rows * SECW)
    coupled = jnp.einsum('hftx,fg->hgtx', grid_block.astype(jnp.float32), couple.astype(jnp.float32))
    tendency = (coupled * factor[:, None, :, :]).astype(jnp.bfloat16)
    tend_rows = tendency.reshape(2, FIELDS, N_SECT, block_rows, SECW).astype(jnp.float32)
    sector_sums = jnp.einsum('hgtrc,rcq->rhtgq', tend_rows, trig_table.astype(jnp.float32))
    cos_part = sector_sums[..., :wave_total]
    sin_part = sector_sums[..., wave_total:]
    real_sum = lax.optimization_barrier(jnp.sum(cos_wide * cos_part + sin_wide * sin_part, axis=2))
    imag_sum = lax.optimization_barrier(jnp.sum(cos_wide * sin_part - sin_wide * cos_part, axis=2))
    inverse_scale = 2.0 / (synth_scale * lengths)
    analysis = jnp.stack([real_sum, imag_sum], axis=2) * inverse_scale[:, None, None, None, None]
    resolved = 2 * wave_list[None, :] < band_points[:, None]
    analysis = jnp.where(resolved[:, None, None, None, :], analysis, 0.0).astype(jnp.bfloat16)
    return (grid_block, jnp.transpose(analysis, (4, 1, 2, 3, 0)))

def reference(spec_in, pair_low, row_points, legendre, gauss_weight, couple, point_factor):
    leading, odd_parity = slot_tables(pair_low, NMAX)
    spread_coeffs = spread_spectral(spec_in, leading, odd_parity)
    fourier = jnp.einsum('pehrfs,psj->pehrfj', spread_coeffs.astype(jnp.float32), legendre.astype(jnp.float32))
    wave_pairs = jnp.stack([pair_low, NMAX - pair_low], axis=1)
    resolved = 2 * wave_pairs[:, :, None] < row_points[None, None, :]
    fourier = jnp.where(resolved[:, :, None, None, None, :], fourier, 0.0).astype(jnp.bfloat16)
    wave_total = 2 * NPAIR
    fourier = fourier.reshape(wave_total, 2, 2, FIELDS, NROWH)
    wave_list = wave_pairs.reshape(-1)
    block_count = NROWH // 16
    synth_scale = 2.0 / math.sqrt(2.0 * NMAX * NPAIR)
    four_blocks = jnp.transpose(fourier.reshape(wave_total, 2, 2, FIELDS, block_count, 16), (4, 0, 1, 2, 3, 5))
    point_blocks = row_points.reshape(block_count, 16)
    factor_blocks = jnp.transpose(point_factor.reshape(2, N_SECT, block_count, 16 * SECW), (2, 0, 1, 3))

    def one_block(inputs):
        return block_step(inputs[0], inputs[1], inputs[2], wave_list, couple, synth_scale)
    grid_blocks, analysis_blocks = lax.map(one_block, (four_blocks, point_blocks, factor_blocks))
    grid_field = jnp.transpose(grid_blocks, (1, 2, 3, 0, 4)).reshape(2, FIELDS, N_SECT, NROWH * SECW)
    analysis = jnp.transpose(analysis_blocks, (1, 2, 3, 4, 0, 5)).reshape(NPAIR, 2, 2, 2, FIELDS, NROWH).astype(jnp.float32)
    north_half = analysis[:, :, 0]
    south_half = analysis[:, :, 1]
    weighted = jnp.stack([(north_half + south_half) * gauss_weight, (north_half - south_half) * gauss_weight], axis=2).astype(jnp.bfloat16)
    projected = jnp.einsum('peorfj,psj->peorfs', weighted.astype(jnp.float32), legendre.astype(jnp.float32))
    member_low = jnp.where(odd_parity[:, None, None, :], projected[:, 0, 1], projected[:, 0, 0])
    member_high = jnp.where(odd_parity[:, None, None, :], projected[:, 1, 1], projected[:, 1, 0])
    spec_out = jnp.where(leading[:, None, None, :], member_low, member_high)
    return (grid_field, spec_out)
```

```python
import functools
import math

import jax
import jax.numpy as jnp
from jax import lax
from jax.experimental import pallas as pl
from jax.experimental.pallas import tpu as pltpu
from jax.sharding import Mesh
from jax.sharding import PartitionSpec as P

WAVE = ("wave_0", "wave_1")
NMAX = 640
ROWS = 40
SECW = 41
NSECT = 64
BANDS = 16
LANES = 128
GROUPS = 8
GROUP_ROWS = [[g, 15 - g, 16 + g, 31 - g, 32 + g] for g in range(GROUPS)]
SCALE = 2.0 / math.sqrt(40960.0)
F32 = jnp.float32
BF16 = jnp.bfloat16
SMEM = pltpu.SMEM


def lane_iota(shape):
    return lax.broadcasted_iota(jnp.int32, shape, len(shape) - 1)


def sincos_quarter(product, quarter):
    inverse = 1.0 / quarter
    turns = jnp.floor(product * inverse + 0.5)
    rest = product - turns * quarter
    theta = rest * (inverse * (0.5 * math.pi))
    sq = theta * theta
    sin_poly = theta + theta * sq * (
        -1.6666667163e-1 + sq * (8.3333337680e-3 + sq * (-1.9841270114e-4 + sq * 2.7557314297e-6))
    )
    cos_poly = 1.0 + sq * (
        -0.5 + sq * (4.1666667908e-2 + sq * (-1.3888889225e-3 + sq * (2.4801587642e-5 - sq * 2.7557314297e-7)))
    )
    return turns.astype(jnp.int32), cos_poly, sin_poly


def turn_cos(turn, cos_poly, sin_poly):
    value = jnp.where((turn & 1) == 1, sin_poly, cos_poly)
    return jnp.where(((turn + 1) & 2) == 2, -value, value)


def wave_lanes(low_ref, shape):
    lane = lane_iota(shape)
    low = jnp.zeros(shape, jnp.int32)
    for pair in range(32):
        low = jnp.where((lane >> 2) == pair, low_ref[pair], low)
    return jnp.where(((lane >> 1) & 1) == 0, low, NMAX - low)


def group_offsets(points_ref, first, group):
    found = []
    offset = jnp.int32(0)
    for row in GROUP_ROWS[group]:
        points = points_ref[first + row]
        width = (points + (NSECT - 1)) >> 6
        found.append((row, points, width, offset))
        offset = offset + width
    return found


def tables_kernel(rank_ref, low_ref, points_ref, factor_ref, u_ref, w_ref, trig_ref, slot_ref, pf_ref, scale_ref, pad_ref):
    first = rank_ref[0] * ROWS
    waves = wave_lanes(low_ref, (8, LANES))
    waves_f = waves.astype(F32)
    lane = lane_iota((NSECT, LANES))
    even = (lane & 1) == 0
    even_row = (lane_iota((1, LANES)) & 1) == 0
    sector = lax.broadcasted_iota(jnp.int32, (NSECT, LANES), 0).astype(F32)
    wave_row = waves_f[0:1]
    scale_ref[...] = jnp.zeros((LANES, LANES), F32)
    for half in range(ROWS // 2):
        row_a, row_b = 2 * half, 2 * half + 1
        points = jnp.where(even_row, points_ref[first + row_a], points_ref[first + row_b])
        width = (points + (NSECT - 1)) >> 6
        quarter = points.astype(F32) * 0.25
        step = wave_row * width.astype(F32)
        turn, cos_poly, sin_poly = sincos_quarter(sector * step, jnp.broadcast_to(quarter, (NSECT, LANES)))
        cos_ab = turn_cos(turn, cos_poly, sin_poly)
        sin_ab = turn_cos(turn + 3, cos_poly, sin_poly)
        cos_up = pltpu.roll(cos_ab, 1, axis=1)
        sin_up = pltpu.roll(sin_ab, 1, axis=1)
        cos_down = pltpu.roll(cos_ab, LANES - 1, axis=1)
        sin_down = pltpu.roll(sin_ab, LANES - 1, axis=1)
        u_ref[row_a] = jnp.where(even, cos_ab, sin_up)
        w_ref[row_a] = jnp.where(even, -sin_ab, cos_up)
        u_ref[row_b] = jnp.where(even, cos_down, sin_ab)
        w_ref[row_b] = jnp.where(even, -sin_down, cos_ab)
        for row in (row_a, row_b):
            length = jnp.full((1, LANES), points_ref[first + row], jnp.int32)
            keep = jnp.where(2 * waves[0:1] < length, (2.0 / SCALE) / length.astype(F32), 0.0)
            scale_ref[row : row + 1, :] = keep
            scale_ref[64 + row : 65 + row, :] = keep
    wave_col = jnp.transpose(jnp.broadcast_to(wave_row, (LANES, LANES)))
    part = lax.broadcasted_iota(jnp.int32, (LANES, LANES), 0) & 1
    slot = lane_iota((1, LANES))
    for h in range(2):
        pad_ref[h : h + 1, 0 : ROWS * SECW] = factor_ref[h]
    for group in range(GROUPS):
        which = jnp.full((1, LANES), -1, jnp.int32)
        column = jnp.zeros((1, LANES), jnp.int32)
        points = jnp.full((1, LANES), 20, jnp.int32)
        width = jnp.zeros((1, LANES), jnp.int32)
        packed = [jnp.zeros((1, LANES), F32), jnp.zeros((1, LANES), F32)]
        for i, (row, row_points, row_width, offset) in enumerate(group_offsets(points_ref, first, group)):
            mine = (slot >= offset) & (slot < offset + row_width)
            which = jnp.where(mine, i, which)
            column = jnp.where(mine, slot - offset, column)
            points = jnp.where(mine, row_points, points)
            width = jnp.where(mine, row_width, width)
            start = row * SECW
            base, shift = (start // LANES) * LANES, start % LANES
            for h in range(2):
                window = jnp.broadcast_to(pad_ref[h : h + 1, base : base + 2 * LANES], (8, 2 * LANES))
                window = pltpu.roll(window, 2 * LANES - shift, axis=1)[:, 0:LANES]
                window = pltpu.roll(window, offset & (LANES - 1), axis=1)
                packed[h] = jnp.where(mine, window[0:1], packed[h])
        slot_ref[0, group : group + 1, :] = which
        slot_ref[1, group : group + 1, :] = width
        slot_ref[2, group : group + 1, :] = points - column
        for h in range(2):
            pf_ref[h * GROUPS + group : h * GROUPS + group + 1, :] = packed[h]
        quarter = jnp.broadcast_to(points.astype(F32) * 0.25, (LANES, LANES))
        turn, cos_poly, sin_poly = sincos_quarter(wave_col * column.astype(F32), quarter)
        trig_ref[group] = turn_cos(turn + part, cos_poly, sin_poly).astype(BF16)


def synth_kernel(block_ref, u_ref, w_ref, trig_ref, slot_ref, out_ref, a_ref, b_ref, lhs_ref, row_ref):
    even = (lane_iota((LANES, LANES)) & 1) == 0
    coeffs = jnp.transpose(block_ref[...].astype(F32)) * SCALE
    a_ref[...] = jnp.where(even, coeffs, pltpu.roll(coeffs, 1, axis=1))
    b_ref[...] = jnp.where(even, pltpu.roll(coeffs, LANES - 1, axis=1), coeffs)
    sector = lax.broadcasted_iota(jnp.int32, (NSECT, LANES), 0)
    for group in range(GROUPS):
        for i, row in enumerate(GROUP_ROWS[group]):
            u = u_ref[row]
            w = w_ref[row]
            for h in range(2):
                at = h * 64 + row
                rot = a_ref[at : at + 1, :] * u + b_ref[at : at + 1, :] * w
                place = (i * 2 + h) * NSECT
                lhs_ref[place : place + NSECT, :] = rot.astype(BF16)
        product = jnp.dot(lhs_ref[...], trig_ref[group], preferred_element_type=F32)
        which = slot_ref[0, group : group + 1, :]
        valid = sector * slot_ref[1, group : group + 1, :] < slot_ref[2, group : group + 1, :]
        which = jnp.where(valid, which, -1)
        for h in range(2):
            total = jnp.zeros((NSECT, LANES), F32)
            for i in range(5):
                place = (i * 2 + h) * NSECT
                total = jnp.where(which == i, product[place : place + NSECT, :], total)
            row_ref[pl.ds(h * GROUPS + group, NSECT, stride=2 * GROUPS), :] = total
    out_ref[...] = row_ref[...].astype(BF16)


def tendency_kernel(grid_ref, couple_ref, pf_ref, out_ref, row_ref):
    row_ref[...] = grid_ref[...].astype(F32)
    couple = jnp.transpose(couple_ref[...].astype(F32)).astype(BF16)
    tends = []
    for line in range(2 * GROUPS):
        values = row_ref[pl.ds(line, NSECT, stride=2 * GROUPS), :].astype(BF16)
        coupled = jnp.dot(couple, values, preferred_element_type=F32)
        tends.append(coupled * pf_ref[line : line + 1, :])
    for line in range(2 * GROUPS):
        row_ref[pl.ds(line, NSECT, stride=2 * GROUPS), :] = tends[line]
    out_ref[...] = row_ref[...].astype(BF16)


def expand_kernel(rank_ref, points_ref, grid_ref, out_ref, row_ref, wide_ref):
    first = rank_ref[0] * ROWS
    row_ref[...] = grid_ref[...].astype(F32)
    lane = lane_iota((NSECT, LANES))
    tiles = -(-ROWS * SECW // LANES)
    info = {}
    for group in range(GROUPS):
        for row, _, width, offset in group_offsets(points_ref, first, group):
            info[row] = (group, width, offset)
    for h in range(2):
        for tile in range(tiles):
            total = jnp.zeros((NSECT, LANES), F32)
            for row in range(ROWS):
                start = row * SECW - tile * LANES
                if start >= LANES or start + SECW <= 0:
                    continue
                group, width, offset = info[row]
                values = row_ref[pl.ds(h * GROUPS + group, NSECT, stride=2 * GROUPS), :]
                values = pltpu.roll(values, (start + 2 * LANES - offset) & (LANES - 1), axis=1)
                total = jnp.where((lane >= start) & (lane < start + width), values, total)
            wide_ref[:, tile * LANES : (tile + 1) * LANES] = total
        out_ref[h] = wide_ref[:, 0 : ROWS * SECW].astype(BF16)


def analysis_kernel(tend_ref, u_ref, w_ref, trig_ref, slot_ref, scale_ref, out_ref, row_ref, lhs_ref, yu_ref, yw_ref):
    row_ref[...] = tend_ref[...].astype(F32)
    yu_ref[...] = jnp.zeros((LANES, LANES), F32)
    yw_ref[...] = jnp.zeros((LANES, LANES), F32)
    for group in range(GROUPS):
        which = slot_ref[0, group : group + 1, :]
        for h in range(2):
            values = row_ref[pl.ds(h * GROUPS + group, NSECT, stride=2 * GROUPS), :]
            for i in range(5):
                place = (i * 2 + h) * NSECT
                lhs_ref[place : place + NSECT, :] = jnp.where(which == i, values, 0.0).astype(BF16)
        product = lax.dot_general(
            lhs_ref[...], trig_ref[group], (((1,), (1,)), ((), ())), preferred_element_type=F32
        )
        for i, row in enumerate(GROUP_ROWS[group]):
            u = u_ref[row]
            w = w_ref[row]
            for h in range(2):
                place = (i * 2 + h) * NSECT
                sums = product[place : place + NSECT, :]
                at = h * 64 + row
                yu_ref[at : at + 1, :] = jnp.sum(sums * u, axis=0, keepdims=True)
                yw_ref[at : at + 1, :] = jnp.sum(sums * w, axis=0, keepdims=True)
    even = (lane_iota((LANES, LANES)) & 1) == 0
    yu = yu_ref[...]
    yw = yw_ref[...]
    real = yu + pltpu.roll(yu, LANES - 1, axis=1)
    imag = yw + pltpu.roll(yw, 1, axis=1)
    result = jnp.where(even, real, imag) * scale_ref[...]
    out_ref[...] = jnp.transpose(result).astype(BF16)


def slot_signs(low, shape):
    slot = lane_iota(shape)
    leading = slot < NMAX - low
    odd = jnp.where(leading, slot & 1, (slot + low) & 1) == 1
    return leading, odd


def legendre_kernel(rank_ref, low_ref, points_ref, spec_ref, leg_ref, out_ref, wide_ref):
    line = lax.broadcasted_iota(jnp.int32, (8, NMAX), 0)
    h = line >> 2
    member = (line >> 1) & 1
    part = line & 1
    points = points_ref[...]
    found = []
    for p in range(2):
        low = low_ref[2 * rank_ref[0] + p]
        leading, odd = slot_signs(low, (8, NMAX))
        spec = spec_ref[p].astype(F32)
        value = jnp.where(part == 0, spec[0:1], spec[1:2])
        value = jnp.where((member == 0) == leading, value, 0.0)
        value = jnp.where((h == 1) & odd, -value, value)
        product = jnp.dot(value.astype(BF16), leg_ref[p], preferred_element_type=F32)
        wave = jnp.where(member == 0, low, NMAX - low)
        found.append(jnp.where(2 * wave < points, product, 0.0))
    upper = line < 4
    wide_ref[...] = jnp.zeros((16, 6 * LANES), F32)
    wide_ref[0:8, 0:NMAX] = jnp.where(upper, found[0], pltpu.roll(found[1], 4, axis=0))
    wide_ref[8:16, 0:NMAX] = jnp.where(upper, pltpu.roll(found[0], 4, axis=0), found[1])
    lane = lane_iota((8, LANES))
    for band in range(BANDS):
        start = band * ROWS
        base, shift = (start // LANES) * LANES, start % LANES
        window = wide_ref[:, base : base + 2 * LANES]
        north = pltpu.roll(window[0:8], (2 * LANES - shift) % (2 * LANES), axis=1)[:, 0:LANES]
        south = pltpu.roll(window[8:16], (2 * LANES + 64 - shift) % (2 * LANES), axis=1)[:, 0:LANES]
        out_ref[band] = jnp.where(lane < 64, north, south).astype(BF16)


def project_kernel(rank_ref, low_ref, back_ref, gauss_ref, leg_ref, out_ref, wide_ref):
    lane = lane_iota((8, LANES))
    for tile in range(NMAX // LANES):
        north = jnp.zeros((8, LANES), F32)
        south = jnp.zeros((8, LANES), F32)
        for band in range(BANDS):
            start = band * ROWS - tile * LANES
            if start >= LANES or start + ROWS <= 0:
                continue
            block = back_ref[band].astype(F32)
            mine = (lane >= start) & (lane < start + ROWS)
            north = jnp.where(mine, pltpu.roll(block, start % LANES, axis=1), north)
            south = jnp.where(mine, pltpu.roll(block, (start + 64) % LANES, axis=1), south)
        wide_ref[0:8, tile * LANES : (tile + 1) * LANES] = north
        wide_ref[8:16, tile * LANES : (tile + 1) * LANES] = south
    north = wide_ref[0:8, :]
    south = wide_ref[8:16, :]
    gauss = gauss_ref[...]
    both = (north + south) * gauss
    less = (north - south) * gauss
    upper = lax.broadcasted_iota(jnp.int32, (8, NMAX), 0) < 4
    forms = [
        jnp.where(upper, both, pltpu.roll(less, 4, axis=0)),
        jnp.where(upper, pltpu.roll(both, 4, axis=0), less),
    ]
    for p in range(2):
        low = low_ref[2 * rank_ref[0] + p]
        leading, odd = slot_signs(low, (1, NMAX))
        product = lax.dot_general(
            forms[p].astype(BF16), leg_ref[p], (((1,), (1,)), ((), ())), preferred_element_type=F32
        )
        for r in range(2):
            lower = jnp.where(odd, product[4 + r : 5 + r], product[r : r + 1])
            higher = jnp.where(odd, product[6 + r : 7 + r], product[2 + r : 3 + r])
            out_ref[2 * p + r] = jnp.where(leading, lower, higher)


def whole():
    return pl.BlockSpec(memory_space=pltpu.VMEM)


def scalars():
    return pl.BlockSpec(memory_space=SMEM)


def run(kernel, name, outs, in_specs, scratch, *args):
    many = isinstance(outs, (list, tuple))
    return pl.pallas_call(
        kernel,
        out_shape=outs,
        in_specs=in_specs,
        out_specs=[whole() for _ in outs] if many else whole(),
        scratch_shapes=scratch,
        name=name,
    )(*args)


def struct(shape, dtype):
    return jax.ShapeDtypeStruct(shape, dtype)


def vmem(shape, dtype):
    return pltpu.VMEM(shape, dtype)


def make_tables(rank, pair_low, row_points, point_factor):
    return run(
        tables_kernel,
        "tables",
        [
            struct((ROWS, NSECT, LANES), F32),
            struct((ROWS, NSECT, LANES), F32),
            struct((GROUPS, LANES, LANES), BF16),
            struct((3, GROUPS, LANES), jnp.int32),
            struct((2 * GROUPS, LANES), F32),
            struct((LANES, LANES), F32),
        ],
        [scalars(), scalars(), scalars(), whole()],
        [vmem((8, 14 * LANES), F32)],
        rank, pair_low, row_points, point_factor,
    )


def synthesize(block, u, w, trig, slots):
    return run(
        synth_kernel,
        "synth",
        struct((NSECT * 2 * GROUPS, LANES), BF16),
        [whole()] * 5,
        [
            vmem((LANES, LANES), F32),
            vmem((LANES, LANES), F32),
            vmem((10 * NSECT, LANES), BF16),
            vmem((NSECT * 2 * GROUPS, LANES), F32),
        ],
        block.reshape(LANES, LANES), u, w, trig, slots,
    ).reshape(NSECT, 2 * GROUPS, LANES)


def tend_of(grid, couple, pf):
    return run(
        tendency_kernel,
        "tendency",
        struct((NSECT * 2 * GROUPS, LANES), BF16),
        [whole()] * 3,
        [vmem((NSECT * 2 * GROUPS, LANES), F32)],
        grid.reshape(-1, LANES), couple, pf,
    ).reshape(NSECT, 2 * GROUPS, LANES)


def expand(rank, row_points, grid):
    return run(
        expand_kernel,
        "expand",
        struct((2, NSECT, ROWS * SECW), BF16),
        [scalars(), scalars(), whole()],
        [vmem((NSECT * 2 * GROUPS, LANES), F32), vmem((NSECT, 13 * LANES), F32)],
        rank, row_points, grid.reshape(-1, LANES),
    )


def analyse(tend, u, w, trig, slots, scale):
    return run(
        analysis_kernel,
        "analysis",
        struct((LANES, LANES), BF16),
        [whole()] * 6,
        [
            vmem((NSECT * 2 * GROUPS, LANES), F32),
            vmem((10 * NSECT, LANES), BF16),
            vmem((LANES, LANES), F32),
            vmem((LANES, LANES), F32),
        ],
        tend.reshape(-1, LANES), u, w, trig, slots, scale,
    ).reshape(BANDS, 8, LANES)


def to_bands(rank, pair_low, row_points, spec, legendre):
    return run(
        legendre_kernel,
        "legendre",
        struct((BANDS, 8, LANES), BF16),
        [scalars(), scalars(), whole(), whole(), whole()],
        [vmem((16, 6 * LANES), F32)],
        rank, pair_low, row_points[None, :], spec, legendre,
    )


def project(rank, pair_low, back, gauss_weight, legendre):
    return run(
        project_kernel,
        "project",
        struct((4, 1, NMAX), F32),
        [scalars(), scalars(), whole(), whole(), whole()],
        [vmem((16, NMAX), F32)],
        rank, pair_low, back, gauss_weight[None, :], legendre,
    )


def cos_sin(product, points):
    quarter = points.astype(F32)[:, None, None] * 0.25
    turn, cos_poly, sin_poly = sincos_quarter(product.astype(F32), quarter)
    return turn_cos(turn, cos_poly, sin_poly), turn_cos(turn + 3, cos_poly, sin_poly)


def loose_path(block, rank, pair_low, row_points, couple, point_factor):
    fourier = block.reshape(BANDS, 2, 2, 2, 2, 64)[..., :ROWS]
    fourier = jnp.transpose(fourier, (0, 1, 2, 4, 3, 5)).reshape(64, 2, 2, ROWS).astype(F32)
    wave_list = jnp.stack([pair_low, NMAX - pair_low], axis=1).reshape(-1)
    points = lax.dynamic_slice_in_dim(row_points, rank[0] * ROWS, ROWS)
    width = (points + NSECT - 1) // NSECT
    columns = jnp.arange(SECW, dtype=jnp.int32)
    cos_inner, sin_inner = cos_sin(wave_list[None, None, :] * columns[None, :, None], points)
    trig = jnp.concatenate([cos_inner, -sin_inner], axis=2).astype(BF16)
    start = jnp.arange(NSECT, dtype=jnp.int32)[None, :] * width[:, None]
    cos_outer, sin_outer = cos_sin(wave_list[None, None, :] * start[:, :, None], points)
    valid = (columns < width[:, None, None]) & (start[:, :, None] + columns < points[:, None, None])
    real = jnp.transpose(fourier[:, :, 0], (2, 1, 0))[:, :, None]
    imag = jnp.transpose(fourier[:, :, 1], (2, 1, 0))[:, :, None]
    cos_wide, sin_wide = cos_outer[:, None], sin_outer[:, None]
    rotated = SCALE * jnp.concatenate(
        [real * cos_wide - imag * sin_wide, real * sin_wide + imag * cos_wide], axis=3
    )
    tile = jnp.einsum("rhnq,rcq->rhnc", rotated.astype(BF16), trig, preferred_element_type=F32)
    tile = jnp.where(valid[:, None], tile, 0.0).astype(BF16)
    local = jnp.transpose(tile, (2, 1, 0, 3)).reshape(NSECT, 2, ROWS * SECW)
    grid = lax.all_to_all(local, "sect", split_axis=0, concat_axis=0, tiled=True)
    coupled = jnp.einsum("fhx,fg->ghx", grid, couple, preferred_element_type=F32)
    tendency = (coupled * point_factor[None, :, 0]).astype(BF16)
    received = lax.all_to_all(tendency, "sect", split_axis=0, concat_axis=0, tiled=True)
    rows = received.reshape(NSECT, 2, ROWS, SECW)
    sums = jnp.einsum("nhrc,rcq->rhnq", rows, trig, preferred_element_type=F32)
    cos_part, sin_part = sums[..., :64], sums[..., 64:]
    real_sum = jnp.sum(cos_wide * cos_part + sin_wide * sin_part, axis=2)
    imag_sum = jnp.sum(cos_wide * sin_part - sin_wide * cos_part, axis=2)
    summed = jnp.stack([real_sum, imag_sum], axis=3)
    keep = 2 * wave_list[None, :] < points[:, None]
    scale = jnp.where(keep, 2.0 / (SCALE * points.astype(F32))[:, None], 0.0)
    analysis = (summed * scale[:, None, :, None]).astype(BF16)
    analysis = jnp.pad(analysis, ((0, 64 - ROWS), (0, 0), (0, 0), (0, 0)))
    analysis = jnp.transpose(analysis, (2, 3, 1, 0)).reshape(BANDS, 8, LANES)
    return jnp.transpose(grid, (1, 0, 2)), analysis


def rows_fit(row_points):
    width = ((row_points + NSECT - 1) // NSECT).reshape(BANDS, 5, GROUPS)
    total = width[:, 0] + width[:, 1, ::-1] + width[:, 2] + width[:, 3, ::-1] + width[:, 4]
    return jnp.max(total) <= LANES


def per_device(spec_in, pair_low, row_points, legendre, gauss_weight, couple, point_factor):
    rank = lax.axis_index(WAVE).astype(jnp.int32).reshape(1)
    outgoing = to_bands(rank, pair_low, row_points, spec_in[:, :, 0], legendre)
    block = lax.all_to_all(outgoing, WAVE, split_axis=0, concat_axis=0, tiled=True)
    u, w, trig, slots, pf, scale = make_tables(rank, pair_low, row_points, point_factor)

    def packed_path(block):
        local = synthesize(block, u, w, trig, slots)
        grid = lax.all_to_all(local, "sect", split_axis=0, concat_axis=0, tiled=True)
        tend = tend_of(grid, couple, pf)
        received = lax.all_to_all(tend, "sect", split_axis=0, concat_axis=0, tiled=True)
        return expand(rank, row_points, grid), analyse(received, u, w, trig, slots, scale)

    def every_slot(block):
        return loose_path(block, rank, pair_low, row_points, couple, point_factor)

    grid_field, analysis = lax.cond(rows_fit(row_points), packed_path, every_slot, block)
    back = lax.all_to_all(analysis, WAVE, split_axis=0, concat_axis=0, tiled=True)
    spec_out = project(rank, pair_low, back, gauss_weight, legendre)
    return grid_field[:, :, None, :], spec_out.reshape(2, 2, 1, NMAX)


def solution(mesh):
    split = Mesh(mesh.devices.reshape(8, 2, mesh.shape["sect"]), ("wave_0", "wave_1", "sect"))
    in_specs = (
        P(WAVE, None, "sect", None),
        P(),
        P(),
        P(WAVE, None, None),
        P(),
        P(),
        P(None, "sect", WAVE),
    )
    out_specs = (P(None, None, "sect", WAVE), P(WAVE, None, "sect", None))
    return jax.shard_map(
        per_device, mesh=split, in_specs=in_specs, out_specs=out_specs, check_vma=False
    )
```

```python
import functools
import math

import jax
import jax.numpy as jnp
from jax import lax
from jax.experimental import pallas as pl
from jax.experimental.pallas import tpu as pltpu
from jax.sharding import Mesh
from jax.sharding import PartitionSpec as P

WAVE = ("wave_0", "wave_1")
NMAX = 640
ROWS = 40
SECW = 41
NSECT = 64
BANDS = 16
LANES = 128
GROUPS = 8
GROUP_ROWS = [[g, 15 - g, 16 + g, 31 - g, 32 + g] for g in range(GROUPS)]
SCALE = 2.0 / math.sqrt(40960.0)
F32 = jnp.float32
BF16 = jnp.bfloat16
SMEM = pltpu.SMEM
GRANT = 12 * 2**20


def lane_iota(shape):
    return lax.broadcasted_iota(jnp.int32, shape, len(shape) - 1)


COS_TERMS = (6.52745434, -25.9667114, 60.1673855, -85.4501082, 64.9391157, -19.7392045, 0.999999989)
SIN_TERMS = (3.23767246, -14.8995044, 42.0258325, -76.7030033, 81.6051307, -41.3417004, 6.2831853)


def turn_part(product, points):
    inverse = 1.0 / points
    whole_turns = jnp.floor(product * inverse + 0.5)
    return (product - whole_turns * points) * inverse


def series(terms, square):
    value = terms[0] * square + terms[1]
    for term in terms[2:]:
        value = value * square + term
    return value


def cos_turn(turn):
    return series(COS_TERMS, turn * turn)


def sin_turn(turn):
    return turn * series(SIN_TERMS, turn * turn)


def wave_lanes(low_ref, shape):
    lane = lane_iota(shape)
    low = jnp.zeros(shape, jnp.int32)
    for pair in range(32):
        low = jnp.where((lane >> 2) == pair, low_ref[pair], low)
    return jnp.where(((lane >> 1) & 1) == 0, low, NMAX - low)


def group_offsets(points_ref, first, group):
    found = []
    offset = jnp.int32(0)
    for row in GROUP_ROWS[group]:
        points = points_ref[first + row]
        width = (points + (NSECT - 1)) >> 6
        found.append((row, points, width, offset))
        offset = offset + width
    return found


def tables_kernel(rank_ref, low_ref, points_ref, factor_ref, coarse_ref, fine_ref, trig_ref, slot_ref, pf_ref, scale_ref, pad_ref):
    first = rank_ref[0] * ROWS
    waves = wave_lanes(low_ref, (8, LANES))
    waves_f = waves.astype(F32)
    wave_row = waves_f[0:1]
    line = lax.broadcasted_iota(jnp.int32, (8, LANES), 0).astype(F32)
    odd_lane = (lane_iota((8, LANES)) & 1).astype(F32)
    fine_step = waves_f * line
    coarse_step = fine_step * 8.0
    back_quarter = odd_lane * 0.75
    scale_ref[...] = jnp.zeros((LANES, LANES), F32)
    for row in range(ROWS):
        length = jnp.full((8, LANES), points_ref[first + row], jnp.int32)
        points = length.astype(F32)
        width = ((length + (NSECT - 1)) >> 6).astype(F32)
        fine = turn_part(fine_step * width, points)
        fine_ref[0, row] = cos_turn(fine)
        fine_ref[1, row] = sin_turn(fine)
        coarse = turn_part(coarse_step * width + back_quarter * points, points)
        coarse_ref[0, row] = cos_turn(coarse)
        coarse_ref[1, row] = -sin_turn(coarse)
        keep = jnp.where(2 * waves < length, (2.0 / SCALE) / points, 0.0)[0:1]
        scale_ref[row : row + 1, :] = keep
        scale_ref[64 + row : 65 + row, :] = keep
    wave_col = jnp.transpose(jnp.broadcast_to(wave_row, (LANES, LANES)))
    quarter = (lax.broadcasted_iota(jnp.int32, (LANES, LANES), 0) & 1).astype(F32) * 0.25
    slot = lane_iota((1, LANES))
    for h in range(2):
        pad_ref[h : h + 1, 0 : ROWS * SECW] = factor_ref[h]
    for group in range(GROUPS):
        which = jnp.full((1, LANES), -1, jnp.int32)
        column = jnp.zeros((1, LANES), jnp.int32)
        points = jnp.full((1, LANES), 20, jnp.int32)
        width = jnp.zeros((1, LANES), jnp.int32)
        packed = jnp.zeros((8, LANES), F32)
        for i, (row, row_points, row_width, offset) in enumerate(group_offsets(points_ref, first, group)):
            mine = (slot >= offset) & (slot < offset + row_width)
            which = jnp.where(mine, i, which)
            column = jnp.where(mine, slot - offset, column)
            points = jnp.where(mine, row_points, points)
            width = jnp.where(mine, row_width, width)
            start = row * SECW
            base, shift = (start // LANES) * LANES, start % LANES
            window = pltpu.roll(pad_ref[:, base : base + 2 * LANES], 2 * LANES - shift, axis=1)[:, 0:LANES]
            packed = jnp.where(mine, pltpu.roll(window, offset & (LANES - 1), axis=1), packed)
        slot_ref[0, group : group + 1, :] = which
        slot_ref[1, group : group + 1, :] = width
        slot_ref[2, group : group + 1, :] = points - column
        for h in range(2):
            pf_ref[h, group : group + 1, :] = packed[h : h + 1]
        points = jnp.broadcast_to(points.astype(F32), (LANES, LANES))
        turn = turn_part(wave_col * column.astype(F32) + quarter * points, points)
        trig_ref[group] = cos_turn(turn).astype(BF16)


def synth_kernel(block_ref, coarse_ref, fine_ref, trig_ref, slot_ref, scale_ref, out_ref, a_ref, b_ref, lhs_ref, row_ref):
    even = (lane_iota((LANES, LANES)) & 1) == 0
    coeffs = jnp.transpose(block_ref[...].reshape(LANES, LANES).astype(F32))
    coeffs = jnp.where(scale_ref[...] > 0.0, coeffs, 0.0) * SCALE
    a_ref[...] = jnp.where(even, coeffs, pltpu.roll(coeffs, 1, axis=1))
    b_ref[...] = jnp.where(even, pltpu.roll(coeffs, LANES - 1, axis=1), coeffs)
    sector = lax.broadcasted_iota(jnp.int32, (NSECT, LANES), 0)
    for group in range(GROUPS):
        for i, row in enumerate(GROUP_ROWS[group]):
            cos = fine_ref[0, row]
            sin = fine_ref[1, row]
            for h in range(2):
                at = h * 64 + row
                a = a_ref[at : at + 1, :]
                b = b_ref[at : at + 1, :]
                near = a * cos - b * sin
                far = a * sin + b * cos
                for block in range(0, 8, 2):
                    pair = [
                        coarse_ref[0, row, k : k + 1, :] * near + coarse_ref[1, row, k : k + 1, :] * far
                        for k in (block, block + 1)
                    ]
                    place = (i * 2 + h) * NSECT + block * 8
                    lhs_ref[place : place + 16, :] = jnp.concatenate(pair, axis=0).astype(BF16)
        product = jnp.dot(lhs_ref[...], trig_ref[group], preferred_element_type=F32)
        which = slot_ref[0, group : group + 1, :]
        valid = sector * slot_ref[1, group : group + 1, :] < slot_ref[2, group : group + 1, :]
        which = jnp.where(valid, which, -1)
        for h in range(2):
            total = jnp.zeros((NSECT, LANES), F32)
            for i in range(5):
                place = (i * 2 + h) * NSECT
                total = jnp.where(which == i, product[place : place + NSECT, :], total)
            row_ref[pl.ds(h * GROUPS + group, NSECT, stride=2 * GROUPS), :] = total
    out_ref[...] = row_ref[...].astype(BF16).reshape(NSECT, 2 * GROUPS, LANES)


def rows_of(ref):
    return ref[...].reshape(NSECT * 2 * GROUPS, LANES).astype(F32)


def tendency_kernel(grid_ref, couple_ref, pf_ref, out_ref, row_ref):
    row_ref[...] = rows_of(grid_ref)
    couple = jnp.transpose(couple_ref[...].astype(F32)).astype(BF16)
    tends = []
    for line in range(2 * GROUPS):
        values = row_ref[pl.ds(line, NSECT, stride=2 * GROUPS), :].astype(BF16)
        coupled = jnp.dot(couple, values, preferred_element_type=F32)
        h, group = divmod(line, GROUPS)
        tends.append(coupled * pf_ref[h, group : group + 1, :])
    for line in range(2 * GROUPS):
        row_ref[pl.ds(line, NSECT, stride=2 * GROUPS), :] = tends[line]
    out_ref[...] = row_ref[...].astype(BF16).reshape(NSECT, 2 * GROUPS, LANES)


def expand_kernel(rank_ref, points_ref, grid_ref, out_ref, row_ref, wide_ref):
    first = rank_ref[0] * ROWS
    row_ref[...] = rows_of(grid_ref)
    lane = lane_iota((NSECT, LANES))
    tiles = -(-ROWS * SECW // LANES)
    info = {}
    for group in range(GROUPS):
        for row, _, width, offset in group_offsets(points_ref, first, group):
            info[row] = (group, width, offset)
    for h in range(2):
        for tile in range(tiles):
            total = jnp.zeros((NSECT, LANES), F32)
            for row in range(ROWS):
                start = row * SECW - tile * LANES
                if start >= LANES or start + SECW <= 0:
                    continue
                group, width, offset = info[row]
                values = row_ref[pl.ds(h * GROUPS + group, NSECT, stride=2 * GROUPS), :]
                values = pltpu.roll(values, (start + 2 * LANES - offset) & (LANES - 1), axis=1)
                total = jnp.where((lane >= start) & (lane < start + width), values, total)
            wide_ref[:, tile * LANES : (tile + 1) * LANES] = total
        out_ref[h] = wide_ref[:, 0 : ROWS * SECW].astype(BF16)


def analysis_kernel(tend_ref, coarse_ref, fine_ref, trig_ref, slot_ref, scale_ref, out_ref, row_ref, lhs_ref, yu_ref, yw_ref):
    row_ref[...] = rows_of(tend_ref)
    yu_ref[...] = jnp.zeros((LANES, LANES), F32)
    yw_ref[...] = jnp.zeros((LANES, LANES), F32)
    for group in range(GROUPS):
        which = slot_ref[0, group : group + 1, :]
        for h in range(2):
            values = row_ref[pl.ds(h * GROUPS + group, NSECT, stride=2 * GROUPS), :]
            for i in range(5):
                place = (i * 2 + h) * NSECT
                lhs_ref[place : place + NSECT, :] = jnp.where(which == i, values, 0.0).astype(BF16)
        product = lax.dot_general(
            lhs_ref[...], trig_ref[group], (((1,), (1,)), ((), ())), preferred_element_type=F32
        )
        for i, row in enumerate(GROUP_ROWS[group]):
            cos = fine_ref[0, row]
            sin = fine_ref[1, row]
            for h in range(2):
                near = jnp.zeros((8, LANES), F32)
                far = jnp.zeros((8, LANES), F32)
                for block in range(8):
                    place = (i * 2 + h) * NSECT + block * 8
                    sums = product[place : place + 8, :]
                    near = near + sums * coarse_ref[0, row, block : block + 1, :]
                    far = far + sums * coarse_ref[1, row, block : block + 1, :]
                at = h * 64 + row
                yu_ref[at : at + 1, :] = jnp.sum(near * cos + far * sin, axis=0, keepdims=True)
                yw_ref[at : at + 1, :] = jnp.sum(far * cos - near * sin, axis=0, keepdims=True)
    even = (lane_iota((LANES, LANES)) & 1) == 0
    yu = yu_ref[...]
    yw = yw_ref[...]
    real = yu + pltpu.roll(yu, LANES - 1, axis=1)
    imag = yw + pltpu.roll(yw, 1, axis=1)
    result = jnp.where(even, real, imag) * scale_ref[...]
    out_ref[...] = jnp.transpose(result).astype(BF16).reshape(BANDS, 8, LANES)


def slot_signs(low, shape):
    slot = lane_iota(shape)
    leading = slot < NMAX - low
    odd = jnp.where(leading, slot & 1, (slot + low) & 1) == 1
    return leading, odd


def legendre_kernel(rank_ref, low_ref, spec_ref, leg_ref, out_ref, wide_ref):
    line = lax.broadcasted_iota(jnp.int32, (8, NMAX), 0)
    h = line >> 2
    member = (line >> 1) & 1
    part = line & 1
    found = []
    for p in range(2):
        low = low_ref[2 * rank_ref[0] + p]
        leading, odd = slot_signs(low, (8, NMAX))
        spec = spec_ref[p].astype(F32)
        value = jnp.where(part == 0, spec[0:1], spec[1:2])
        value = jnp.where((member == 0) == leading, value, 0.0)
        value = jnp.where((h == 1) & odd, -value, value)
        found.append(jnp.dot(value.astype(BF16), leg_ref[p], preferred_element_type=F32))
    upper = line < 4
    wide_ref[...] = jnp.zeros((16, 6 * LANES), F32)
    wide_ref[0:8, 0:NMAX] = jnp.where(upper, found[0], pltpu.roll(found[1], 4, axis=0))
    wide_ref[8:16, 0:NMAX] = jnp.where(upper, pltpu.roll(found[0], 4, axis=0), found[1])
    lane = lane_iota((8, LANES))
    for band in range(BANDS):
        start = band * ROWS
        base, shift = (start // LANES) * LANES, start % LANES
        window = wide_ref[:, base : base + 2 * LANES]
        north = pltpu.roll(window[0:8], (2 * LANES - shift) % (2 * LANES), axis=1)[:, 0:LANES]
        south = pltpu.roll(window[8:16], (2 * LANES + 64 - shift) % (2 * LANES), axis=1)[:, 0:LANES]
        out_ref[band] = jnp.where(lane < 64, north, south).astype(BF16)


def project_kernel(rank_ref, low_ref, back_ref, gauss_ref, leg_ref, out_ref, wide_ref):
    lane = lane_iota((8, LANES))
    for tile in range(NMAX // LANES):
        north = jnp.zeros((8, LANES), F32)
        south = jnp.zeros((8, LANES), F32)
        for band in range(BANDS):
            start = band * ROWS - tile * LANES
            if start >= LANES or start + ROWS <= 0:
                continue
            block = back_ref[band].astype(F32)
            mine = (lane >= start) & (lane < start + ROWS)
            north = jnp.where(mine, pltpu.roll(block, start % LANES, axis=1), north)
            south = jnp.where(mine, pltpu.roll(block, (start + 64) % LANES, axis=1), south)
        wide_ref[0:8, tile * LANES : (tile + 1) * LANES] = north
        wide_ref[8:16, tile * LANES : (tile + 1) * LANES] = south
    north = wide_ref[0:8, :]
    south = wide_ref[8:16, :]
    gauss = gauss_ref[...]
    both = (north + south) * gauss
    less = (north - south) * gauss
    upper = lax.broadcasted_iota(jnp.int32, (8, NMAX), 0) < 4
    forms = [
        jnp.where(upper, both, pltpu.roll(less, 4, axis=0)),
        jnp.where(upper, pltpu.roll(both, 4, axis=0), less),
    ]
    for p in range(2):
        low = low_ref[2 * rank_ref[0] + p]
        leading, odd = slot_signs(low, (1, NMAX))
        product = lax.dot_general(
            forms[p].astype(BF16), leg_ref[p], (((1,), (1,)), ((), ())), preferred_element_type=F32
        )
        for r in range(2):
            lower = jnp.where(odd, product[4 + r : 5 + r], product[r : r + 1])
            higher = jnp.where(odd, product[6 + r : 7 + r], product[2 + r : 3 + r])
            out_ref[2 * p + r] = jnp.where(leading, lower, higher)


def whole():
    return pl.BlockSpec(memory_space=pltpu.VMEM)


def scalars():
    return pl.BlockSpec(memory_space=SMEM)


def run(kernel, name, outs, in_specs, scratch, *args):
    many = isinstance(outs, (list, tuple))
    return pl.pallas_call(
        kernel,
        out_shape=outs,
        in_specs=in_specs,
        out_specs=[whole() for _ in outs] if many else whole(),
        scratch_shapes=scratch,
        compiler_params=pltpu.CompilerParams(vmem_limit_bytes=GRANT),
        name=name,
    )(*args)


def struct(shape, dtype):
    return jax.ShapeDtypeStruct(shape, dtype)


def vmem(shape, dtype):
    return pltpu.VMEM(shape, dtype)


def make_tables(rank, pair_low, row_points, point_factor):
    return run(
        tables_kernel,
        "tables",
        [
            struct((2, ROWS, 8, LANES), F32),
            struct((2, ROWS, 8, LANES), F32),
            struct((GROUPS, LANES, LANES), BF16),
            struct((3, GROUPS, LANES), jnp.int32),
            struct((2, GROUPS, LANES), F32),
            struct((LANES, LANES), F32),
        ],
        [scalars(), scalars(), scalars(), whole()],
        [vmem((8, 14 * LANES), F32)],
        rank, pair_low, row_points, point_factor,
    )


PACKED = (NSECT, 2 * GROUPS, LANES)
LINES = NSECT * 2 * GROUPS


def synthesize(block, coarse, fine, trig, slots, scale):
    return run(
        synth_kernel,
        "synth",
        struct(PACKED, BF16),
        [whole()] * 6,
        [
            vmem((LANES, LANES), F32),
            vmem((LANES, LANES), F32),
            vmem((10 * NSECT, LANES), BF16),
            vmem((LINES, LANES), F32),
        ],
        block, coarse, fine, trig, slots, scale,
    )


def tend_of(grid, couple, pf):
    return run(
        tendency_kernel,
        "tendency",
        struct(PACKED, BF16),
        [whole()] * 3,
        [vmem((LINES, LANES), F32)],
        grid, couple, pf,
    )


def expand(rank, row_points, grid):
    return run(
        expand_kernel,
        "expand",
        struct((2, NSECT, ROWS * SECW), BF16),
        [scalars(), scalars(), whole()],
        [vmem((LINES, LANES), F32), vmem((NSECT, 13 * LANES), F32)],
        rank, row_points, grid,
    )


def analyse(tend, coarse, fine, trig, slots, scale):
    return run(
        analysis_kernel,
        "analysis",
        struct((BANDS, 8, LANES), BF16),
        [whole()] * 6,
        [
            vmem((LINES, LANES), F32),
            vmem((10 * NSECT, LANES), BF16),
            vmem((LANES, LANES), F32),
            vmem((LANES, LANES), F32),
        ],
        tend, coarse, fine, trig, slots, scale,
    )


def to_bands(rank, pair_low, spec, legendre):
    return run(
        legendre_kernel,
        "legendre",
        struct((BANDS, 8, LANES), BF16),
        [scalars(), scalars(), whole(), whole()],
        [vmem((16, 6 * LANES), F32)],
        rank, pair_low, spec, legendre,
    )


def project(rank, pair_low, back, gauss_weight, legendre):
    return run(
        project_kernel,
        "project",
        struct((4, 1, NMAX), F32),
        [scalars(), scalars(), whole(), whole(), whole()],
        [vmem((16, NMAX), F32)],
        rank, pair_low, back, gauss_weight[None, :], legendre,
    )


def cos_sin(product, points):
    turn = turn_part(product.astype(F32), points.astype(F32)[:, None, None])
    return cos_turn(turn), sin_turn(turn)


def loose_path(block, rank, pair_low, row_points, couple, point_factor):
    fourier = block.reshape(BANDS, 2, 2, 2, 2, 64)[..., :ROWS]
    fourier = jnp.transpose(fourier, (0, 1, 2, 4, 3, 5)).reshape(64, 2, 2, ROWS).astype(F32)
    wave_list = jnp.stack([pair_low, NMAX - pair_low], axis=1).reshape(-1)
    points = lax.dynamic_slice_in_dim(row_points, rank[0] * ROWS, ROWS)
    width = (points + NSECT - 1) // NSECT
    columns = jnp.arange(SECW, dtype=jnp.int32)
    cos_inner, sin_inner = cos_sin(wave_list[None, None, :] * columns[None, :, None], points)
    trig = jnp.concatenate([cos_inner, -sin_inner], axis=2).astype(BF16)
    start = jnp.arange(NSECT, dtype=jnp.int32)[None, :] * width[:, None]
    cos_outer, sin_outer = cos_sin(wave_list[None, None, :] * start[:, :, None], points)
    valid = (columns < width[:, None, None]) & (start[:, :, None] + columns < points[:, None, None])
    keep = 2 * wave_list[None, :] < points[:, None]
    fourier = jnp.where(jnp.transpose(keep)[:, None, None], fourier, 0.0)
    real = jnp.transpose(fourier[:, :, 0], (2, 1, 0))[:, :, None]
    imag = jnp.transpose(fourier[:, :, 1], (2, 1, 0))[:, :, None]
    cos_wide, sin_wide = cos_outer[:, None], sin_outer[:, None]
    rotated = SCALE * jnp.concatenate(
        [real * cos_wide - imag * sin_wide, real * sin_wide + imag * cos_wide], axis=3
    )
    tile = jnp.einsum("rhnq,rcq->rhnc", rotated.astype(BF16), trig, preferred_element_type=F32)
    tile = jnp.where(valid[:, None], tile, 0.0).astype(BF16)
    local = jnp.transpose(tile, (2, 1, 0, 3)).reshape(NSECT, 2, ROWS * SECW)
    grid = lax.all_to_all(local, "sect", split_axis=0, concat_axis=0, tiled=True)
    coupled = jnp.einsum("fhx,fg->ghx", grid, couple, preferred_element_type=F32)
    tendency = (coupled * point_factor[None, :, 0]).astype(BF16)
    received = lax.all_to_all(tendency, "sect", split_axis=0, concat_axis=0, tiled=True)
    rows = received.reshape(NSECT, 2, ROWS, SECW)
    sums = jnp.einsum("nhrc,rcq->rhnq", rows, trig, preferred_element_type=F32)
    cos_part, sin_part = sums[..., :64], sums[..., 64:]
    real_sum = jnp.sum(cos_wide * cos_part + sin_wide * sin_part, axis=2)
    imag_sum = jnp.sum(cos_wide * sin_part - sin_wide * cos_part, axis=2)
    summed = jnp.stack([real_sum, imag_sum], axis=3)
    scale = jnp.where(keep, 2.0 / (SCALE * points.astype(F32))[:, None], 0.0)
    analysis = (summed * scale[:, None, :, None]).astype(BF16)
    analysis = jnp.pad(analysis, ((0, 64 - ROWS), (0, 0), (0, 0), (0, 0)))
    analysis = jnp.transpose(analysis, (2, 3, 1, 0)).reshape(BANDS, 8, LANES)
    return jnp.transpose(grid, (1, 0, 2)), analysis


def rows_fit(row_points):
    width = ((row_points + NSECT - 1) // NSECT).reshape(BANDS, 5, GROUPS)
    total = width[:, 0] + width[:, 1, ::-1] + width[:, 2] + width[:, 3, ::-1] + width[:, 4]
    return jnp.max(total) <= LANES


def per_device(spec_in, pair_low, row_points, legendre, gauss_weight, couple, point_factor):
    rank = lax.axis_index(WAVE).astype(jnp.int32).reshape(1)
    outgoing = to_bands(rank, pair_low, spec_in[:, :, 0], legendre)
    block = lax.all_to_all(outgoing, WAVE, split_axis=0, concat_axis=0, tiled=True)
    coarse, fine, trig, slots, pf, scale = make_tables(rank, pair_low, row_points, point_factor)

    def cross(x):
        return lax.all_to_all(x, "sect", split_axis=0, concat_axis=0, tiled=True)

    def packed_path(block):
        grid = cross(synthesize(block, coarse, fine, trig, slots, scale))
        received = cross(tend_of(grid, couple, pf))
        return expand(rank, row_points, grid), analyse(received, coarse, fine, trig, slots, scale)

    def every_slot(block):
        return loose_path(block, rank, pair_low, row_points, couple, point_factor)

    grid_field, analysis = lax.cond(rows_fit(row_points), packed_path, every_slot, block)
    back = lax.all_to_all(analysis, WAVE, split_axis=0, concat_axis=0, tiled=True)
    spec_out = project(rank, pair_low, back, gauss_weight, legendre)
    return grid_field[:, :, None, :], spec_out.reshape(2, 2, 1, NMAX)


def solution(mesh):
    split = Mesh(mesh.devices.reshape(8, 2, mesh.shape["sect"]), ("wave_0", "wave_1", "sect"))
    in_specs = (
        P(WAVE, None, "sect", None),
        P(),
        P(),
        P(WAVE, None, None),
        P(),
        P(),
        P(None, "sect", WAVE),
    )
    out_specs = (P(None, None, "sect", WAVE), P(WAVE, None, "sect", None))
    return jax.shard_map(
        per_device, mesh=split, in_specs=in_specs, out_specs=out_specs, check_vma=False
    )
```

```python
import functools
import math

import jax
import jax.numpy as jnp
from jax import lax
from jax.experimental import pallas as pl
from jax.experimental.pallas import tpu as pltpu
from jax.sharding import Mesh
from jax.sharding import PartitionSpec as P

WAVE = ("wave_0", "wave_1")
NMAX = 640
ROWS = 40
SECW = 41
NSECT = 64
BANDS = 16
LANES = 128
GROUP_ROWS = [
    [0, 7, 16, 22, 31, 34],
    [9, 12, 25, 26, 39],
    [2, 10, 15, 20, 29, 36],
    [11, 18, 19, 32, 33],
    [4, 6, 13, 24, 28, 37],
    [1, 8, 14, 23, 30, 35],
    [3, 5, 17, 21, 27, 38],
]
GROUPS = len(GROUP_ROWS)
MOST = max(len(rows) for rows in GROUP_ROWS)
SCALE = 2.0 / math.sqrt(40960.0)
F32 = jnp.float32
BF16 = jnp.bfloat16
SMEM = pltpu.SMEM
GRANT = 12 * 2**20
FULL_GRANT = 60 * 1024 * 2**10


def wave_rank():
    return lax.axis_index(WAVE).astype(jnp.int32)


def lane_iota(shape):
    return lax.broadcasted_iota(jnp.int32, shape, len(shape) - 1)


COS_TERMS = (6.52745434, -25.9667114, 60.1673855, -85.4501082, 64.9391157, -19.7392045, 0.999999989)
SIN_TERMS = (3.23767246, -14.8995044, 42.0258325, -76.7030033, 81.6051307, -41.3417004, 6.2831853)


def turn_part(product, points):
    inverse = 1.0 / points
    whole_turns = jnp.floor(product * inverse + 0.5)
    return (product - whole_turns * points) * inverse


def series(terms, square):
    value = terms[0] * square + terms[1]
    for term in terms[2:]:
        value = value * square + term
    return value


def cos_turn(turn):
    return series(COS_TERMS, turn * turn)


def sin_turn(turn):
    return turn * series(SIN_TERMS, turn * turn)


def wave_lanes(low_ref, shape):
    lane = lane_iota(shape)
    low = jnp.zeros(shape, jnp.int32)
    for pair in range(32):
        low = jnp.where((lane >> 2) == pair, low_ref[pair], low)
    return jnp.where(((lane >> 1) & 1) == 0, low, NMAX - low)


def group_offsets(points_ref, first, group):
    found = []
    offset = jnp.int32(0)
    for row in GROUP_ROWS[group]:
        points = points_ref[first + row]
        width = (points + (NSECT - 1)) >> 6
        found.append((row, points, width, offset))
        offset = offset + width
    return found


def tables_kernel(low_ref, points_ref, factor_ref, coarse_ref, fine_ref, trig_ref, slot_ref, pf_ref, scale_ref, pad_ref):
    first = wave_rank() * ROWS
    waves = wave_lanes(low_ref, (8, LANES))
    waves_f = waves.astype(F32)
    wave_row = waves_f[0:1]
    line = lax.broadcasted_iota(jnp.int32, (8, LANES), 0).astype(F32)
    odd_lane = (lane_iota((8, LANES)) & 1).astype(F32)
    fine_step = waves_f * line
    coarse_step = fine_step * 8.0
    back_quarter = odd_lane * 0.75
    scale_ref[...] = jnp.zeros((LANES, LANES), F32)
    for row in range(ROWS):
        length = jnp.full((8, LANES), points_ref[first + row], jnp.int32)
        points = length.astype(F32)
        width = ((length + (NSECT - 1)) >> 6).astype(F32)
        fine = turn_part(fine_step * width, points)
        fine_ref[0, row] = cos_turn(fine)
        fine_ref[1, row] = sin_turn(fine)
        coarse = turn_part(coarse_step * width + back_quarter * points, points)
        coarse_ref[0, row] = cos_turn(coarse)
        coarse_ref[1, row] = -sin_turn(coarse)
        keep = jnp.where(2 * waves < length, (2.0 / SCALE) / points, 0.0)[0:1]
        scale_ref[row : row + 1, :] = keep
        scale_ref[64 + row : 65 + row, :] = keep
    wave_col = jnp.transpose(jnp.broadcast_to(wave_row, (LANES, LANES)))
    quarter = (lax.broadcasted_iota(jnp.int32, (LANES, LANES), 0) & 1).astype(F32) * 0.25
    slot = lane_iota((1, LANES))
    for h in range(2):
        pad_ref[h : h + 1, 0 : ROWS * SECW] = factor_ref[h]
    for group in range(GROUPS):
        which = jnp.full((1, LANES), -1, jnp.int32)
        column = jnp.zeros((1, LANES), jnp.int32)
        points = jnp.full((1, LANES), 20, jnp.int32)
        width = jnp.zeros((1, LANES), jnp.int32)
        packed = jnp.zeros((8, LANES), F32)
        for i, (row, row_points, row_width, offset) in enumerate(group_offsets(points_ref, first, group)):
            mine = (slot >= offset) & (slot < offset + row_width)
            which = jnp.where(mine, i, which)
            column = jnp.where(mine, slot - offset, column)
            points = jnp.where(mine, row_points, points)
            width = jnp.where(mine, row_width, width)
            start = row * SECW
            base, shift = (start // LANES) * LANES, start % LANES
            window = pltpu.roll(pad_ref[:, base : base + 2 * LANES], 2 * LANES - shift, axis=1)[:, 0:LANES]
            packed = jnp.where(mine, pltpu.roll(window, offset & (LANES - 1), axis=1), packed)
        slot_ref[0, group : group + 1, :] = which
        slot_ref[1, group : group + 1, :] = width
        slot_ref[2, group : group + 1, :] = points - column
        for h in range(2):
            pf_ref[h, group : group + 1, :] = packed[h : h + 1]
        points = jnp.broadcast_to(points.astype(F32), (LANES, LANES))
        turn = turn_part(wave_col * column.astype(F32) + quarter * points, points)
        trig_ref[group] = cos_turn(turn).astype(BF16)


def synth_kernel(block_ref, coarse_ref, fine_ref, trig_ref, slot_ref, scale_ref, out_ref, a_ref, b_ref, lhs_ref, row_ref):
    even = (lane_iota((LANES, LANES)) & 1) == 0
    coeffs = jnp.transpose(block_ref[...].reshape(LANES, LANES).astype(F32))
    coeffs = jnp.where(scale_ref[...] > 0.0, coeffs, 0.0) * SCALE
    a_ref[...] = jnp.where(even, coeffs, pltpu.roll(coeffs, 1, axis=1))
    b_ref[...] = jnp.where(even, pltpu.roll(coeffs, LANES - 1, axis=1), coeffs)
    sector = lax.broadcasted_iota(jnp.int32, (NSECT, LANES), 0)
    for group in range(GROUPS):
        used = 2 * NSECT * len(GROUP_ROWS[group])
        for i, row in enumerate(GROUP_ROWS[group]):
            cos = fine_ref[0, row]
            sin = fine_ref[1, row]
            for h in range(2):
                at = h * 64 + row
                a = a_ref[at : at + 1, :]
                b = b_ref[at : at + 1, :]
                near = a * cos - b * sin
                far = a * sin + b * cos
                for block in range(0, 8, 2):
                    pair = [
                        coarse_ref[0, row, k : k + 1, :] * near + coarse_ref[1, row, k : k + 1, :] * far
                        for k in (block, block + 1)
                    ]
                    place = (i * 2 + h) * NSECT + block * 8
                    lhs_ref[place : place + 16, :] = jnp.concatenate(pair, axis=0).astype(BF16)
        product = jnp.dot(lhs_ref[0:used, :], trig_ref[group], preferred_element_type=F32)
        which = slot_ref[0, group : group + 1, :]
        valid = sector * slot_ref[1, group : group + 1, :] < slot_ref[2, group : group + 1, :]
        which = jnp.where(valid, which, -1)
        for h in range(2):
            total = jnp.zeros((NSECT, LANES), F32)
            for i in range(len(GROUP_ROWS[group])):
                place = (i * 2 + h) * NSECT
                total = jnp.where(which == i, product[place : place + NSECT, :], total)
            row_ref[pl.ds(2 * group + h, NSECT, stride=2 * GROUPS), :] = total
    out_ref[...] = row_ref[...].astype(BF16)


def rows_of(ref):
    return ref[...].astype(F32)


def tendency_kernel(grid_ref, couple_ref, pf_ref, out_ref, row_ref):
    row_ref[...] = rows_of(grid_ref)
    couple = jnp.transpose(couple_ref[...].astype(F32)).astype(BF16)
    tends = []
    for line in range(2 * GROUPS):
        values = row_ref[pl.ds(line, NSECT, stride=2 * GROUPS), :].astype(BF16)
        coupled = jnp.dot(couple, values, preferred_element_type=F32)
        group, h = divmod(line, 2)
        tends.append(coupled * pf_ref[h, group : group + 1, :])
    for line in range(2 * GROUPS):
        row_ref[pl.ds(line, NSECT, stride=2 * GROUPS), :] = tends[line]
    out_ref[...] = row_ref[...].astype(BF16)


def expand_kernel(points_ref, grid_ref, out_ref, row_ref, wide_ref):
    first = wave_rank() * ROWS
    row_ref[...] = rows_of(grid_ref)
    lane = lane_iota((NSECT, LANES))
    tiles = -(-ROWS * SECW // LANES)
    info = {}
    for group in range(GROUPS):
        for row, _, width, offset in group_offsets(points_ref, first, group):
            info[row] = (group, width, offset)
    for h in range(2):
        for tile in range(tiles):
            total = jnp.zeros((NSECT, LANES), F32)
            for row in range(ROWS):
                start = row * SECW - tile * LANES
                if start >= LANES or start + SECW <= 0:
                    continue
                group, width, offset = info[row]
                values = row_ref[pl.ds(2 * group + h, NSECT, stride=2 * GROUPS), :]
                values = pltpu.roll(values, (start + 2 * LANES - offset) & (LANES - 1), axis=1)
                total = jnp.where((lane >= start) & (lane < start + width), values, total)
            wide_ref[:, tile * LANES : (tile + 1) * LANES] = total
        out_ref[h] = wide_ref[:, 0 : ROWS * SECW].astype(BF16)


def analysis_kernel(tend_ref, coarse_ref, fine_ref, trig_ref, slot_ref, scale_ref, out_ref, row_ref, lhs_ref, yu_ref, yw_ref):
    row_ref[...] = rows_of(tend_ref)
    yu_ref[...] = jnp.zeros((LANES, LANES), F32)
    yw_ref[...] = jnp.zeros((LANES, LANES), F32)
    for group in range(GROUPS):
        which = slot_ref[0, group : group + 1, :]
        used = 2 * NSECT * len(GROUP_ROWS[group])
        for h in range(2):
            values = row_ref[pl.ds(2 * group + h, NSECT, stride=2 * GROUPS), :]
            for i in range(len(GROUP_ROWS[group])):
                place = (i * 2 + h) * NSECT
                lhs_ref[place : place + NSECT, :] = jnp.where(which == i, values, 0.0).astype(BF16)
        product = lax.dot_general(
            lhs_ref[0:used, :], trig_ref[group], (((1,), (1,)), ((), ())), preferred_element_type=F32
        )
        for i, row in enumerate(GROUP_ROWS[group]):
            cos = fine_ref[0, row]
            sin = fine_ref[1, row]
            for h in range(2):
                near = jnp.zeros((8, LANES), F32)
                far = jnp.zeros((8, LANES), F32)
                for block in range(8):
                    place = (i * 2 + h) * NSECT + block * 8
                    sums = product[place : place + 8, :]
                    near = near + sums * coarse_ref[0, row, block : block + 1, :]
                    far = far + sums * coarse_ref[1, row, block : block + 1, :]
                at = h * 64 + row
                yu_ref[at : at + 1, :] = jnp.sum(near * cos + far * sin, axis=0, keepdims=True)
                yw_ref[at : at + 1, :] = jnp.sum(far * cos - near * sin, axis=0, keepdims=True)
    even = (lane_iota((LANES, LANES)) & 1) == 0
    yu = yu_ref[...]
    yw = yw_ref[...]
    real = yu + pltpu.roll(yu, LANES - 1, axis=1)
    imag = yw + pltpu.roll(yw, 1, axis=1)
    result = jnp.where(even, real, imag) * scale_ref[...]
    out_ref[...] = jnp.transpose(result).astype(BF16).reshape(BANDS, 8, LANES)


def slot_signs(low, shape):
    slot = lane_iota(shape)
    leading = slot < NMAX - low
    odd = jnp.where(leading, slot & 1, (slot + low) & 1) == 1
    return leading, odd


def legendre_kernel(low_ref, spec_hbm, leg_hbm, out_ref, wide_ref, spec_ref, leg_ref, sems):
    half = NMAX // 2
    spec_copy = pltpu.make_async_copy(spec_hbm, spec_ref, sems.at[4])
    spec_copy.start()
    leg_copies = []
    for p in range(2):
        for part in range(2):
            rows = pl.ds(part * half, half)
            leg_copies.append(
                pltpu.make_async_copy(leg_hbm.at[p, rows], leg_ref.at[p, rows], sems.at[2 * p + part])
            )
            leg_copies[-1].start()
    wide_ref[...] = jnp.zeros((16, 6 * LANES), F32)
    spec_copy.wait()
    line = lax.broadcasted_iota(jnp.int32, (8, NMAX), 0)
    h = line >> 2
    member = (line >> 1) & 1
    part = line & 1
    found = []
    for p in range(2):
        low = low_ref[2 * wave_rank() + p]
        leading, odd = slot_signs(low, (8, NMAX))
        spec = spec_ref[p].astype(F32)
        value = jnp.where(part == 0, spec[0:1], spec[1:2])
        value = jnp.where((member == 0) == leading, value, 0.0)
        value = jnp.where((h == 1) & odd, -value, value)
        leg_copies[2 * p].wait()
        leg_copies[2 * p + 1].wait()
        found.append(jnp.dot(value.astype(BF16), leg_ref[p], preferred_element_type=F32))
    upper = line < 4
    wide_ref[0:8, 0:NMAX] = jnp.where(upper, found[0], pltpu.roll(found[1], 4, axis=0))
    wide_ref[8:16, 0:NMAX] = jnp.where(upper, pltpu.roll(found[0], 4, axis=0), found[1])
    lane = lane_iota((8, LANES))
    for band in range(BANDS):
        start = band * ROWS
        base, shift = (start // LANES) * LANES, start % LANES
        window = wide_ref[:, base : base + 2 * LANES]
        north = pltpu.roll(window[0:8], (2 * LANES - shift) % (2 * LANES), axis=1)[:, 0:LANES]
        south = pltpu.roll(window[8:16], (2 * LANES + 64 - shift) % (2 * LANES), axis=1)[:, 0:LANES]
        out_ref[band] = jnp.where(lane < 64, north, south).astype(BF16)


def project_kernel(low_ref, back_ref, gauss_ref, leg_ref, out_ref, wide_ref):
    lane = lane_iota((8, LANES))
    for tile in range(NMAX // LANES):
        north = jnp.zeros((8, LANES), F32)
        south = jnp.zeros((8, LANES), F32)
        for band in range(BANDS):
            start = band * ROWS - tile * LANES
            if start >= LANES or start + ROWS <= 0:
                continue
            block = back_ref[band].astype(F32)
            mine = (lane >= start) & (lane < start + ROWS)
            north = jnp.where(mine, pltpu.roll(block, start % LANES, axis=1), north)
            south = jnp.where(mine, pltpu.roll(block, (start + 64) % LANES, axis=1), south)
        wide_ref[0:8, tile * LANES : (tile + 1) * LANES] = north
        wide_ref[8:16, tile * LANES : (tile + 1) * LANES] = south
    north = wide_ref[0:8, :]
    south = wide_ref[8:16, :]
    gauss = gauss_ref[...]
    both = (north + south) * gauss
    less = (north - south) * gauss
    upper = lax.broadcasted_iota(jnp.int32, (8, NMAX), 0) < 4
    forms = [
        jnp.where(upper, both, pltpu.roll(less, 4, axis=0)),
        jnp.where(upper, pltpu.roll(both, 4, axis=0), less),
    ]
    for p in range(2):
        low = low_ref[2 * wave_rank() + p]
        leading, odd = slot_signs(low, (1, NMAX))
        product = lax.dot_general(
            forms[p].astype(BF16), leg_ref[p], (((1,), (1,)), ((), ())), preferred_element_type=F32
        )
        for r in range(2):
            lower = jnp.where(odd, product[4 + r : 5 + r], product[r : r + 1])
            higher = jnp.where(odd, product[6 + r : 7 + r], product[2 + r : 3 + r])
            out_ref[2 * p + r] = jnp.where(leading, lower, higher)


def whole():
    return pl.BlockSpec(memory_space=pltpu.VMEM)


def in_hbm():
    return pl.BlockSpec(memory_space=pltpu.HBM)


def scalars():
    return pl.BlockSpec(memory_space=SMEM)


def run(kernel, name, outs, in_specs, scratch, *args, grant=GRANT):
    many = isinstance(outs, (list, tuple))
    return pl.pallas_call(
        kernel,
        out_shape=outs,
        in_specs=in_specs,
        out_specs=[whole() for _ in outs] if many else whole(),
        scratch_shapes=scratch,
        compiler_params=pltpu.CompilerParams(vmem_limit_bytes=grant),
        name=name,
    )(*args)


def struct(shape, dtype):
    return jax.ShapeDtypeStruct(shape, dtype)


def vmem(shape, dtype):
    return pltpu.VMEM(shape, dtype)


def make_tables(pair_low, row_points, point_factor):
    return run(
        tables_kernel,
        "tables",
        [
            struct((2, ROWS, 8, LANES), F32),
            struct((2, ROWS, 8, LANES), F32),
            struct((GROUPS, LANES, LANES), BF16),
            struct((3, GROUPS, LANES), jnp.int32),
            struct((2, GROUPS, LANES), F32),
            struct((LANES, LANES), F32),
        ],
        [scalars(), scalars(), whole()],
        [vmem((8, 14 * LANES), F32)],
        pair_low, row_points, point_factor,
    )


LINES = NSECT * 2 * GROUPS


def synthesize(block, coarse, fine, trig, slots, scale):
    return run(
        synth_kernel,
        "synth",
        struct((LINES, LANES), BF16),
        [whole()] * 6,
        [
            vmem((LANES, LANES), F32),
            vmem((LANES, LANES), F32),
            vmem((2 * MOST * NSECT, LANES), BF16),
            vmem((LINES, LANES), F32),
        ],
        block, coarse, fine, trig, slots, scale,
    )


def tend_of(grid, couple, pf):
    return run(
        tendency_kernel,
        "tendency",
        struct((LINES, LANES), BF16),
        [whole()] * 3,
        [vmem((LINES, LANES), F32)],
        grid, couple, pf,
    )


def expand(row_points, grid):
    return run(
        expand_kernel,
        "expand",
        struct((2, NSECT, ROWS * SECW), BF16),
        [scalars(), whole()],
        [vmem((LINES, LANES), F32), vmem((NSECT, 13 * LANES), F32)],
        row_points, grid,
    )


def analyse(tend, coarse, fine, trig, slots, scale):
    return run(
        analysis_kernel,
        "analysis",
        struct((BANDS, 8, LANES), BF16),
        [whole()] * 6,
        [
            vmem((LINES, LANES), F32),
            vmem((2 * MOST * NSECT, LANES), BF16),
            vmem((LANES, LANES), F32),
            vmem((LANES, LANES), F32),
        ],
        tend, coarse, fine, trig, slots, scale,
    )


def to_bands(pair_low, spec, legendre):
    return run(
        legendre_kernel,
        "legendre",
        struct((BANDS, 8, LANES), BF16),
        [scalars(), in_hbm(), in_hbm()],
        [
            vmem((16, 6 * LANES), F32),
            vmem((2, 2, NMAX), BF16),
            vmem((2, NMAX, NMAX), BF16),
            pltpu.SemaphoreType.DMA((5,)),
        ],
        pair_low, spec, legendre,
        grant=FULL_GRANT,
    )


def project(pair_low, back, gauss_weight, legendre):
    return run(
        project_kernel,
        "project",
        struct((4, 1, NMAX), F32),
        [scalars(), whole(), whole(), whole()],
        [vmem((16, NMAX), F32)],
        pair_low, back, gauss_weight[None, :], legendre,
    )


def cos_sin(product, points):
    turn = turn_part(product.astype(F32), points.astype(F32)[:, None, None])
    return cos_turn(turn), sin_turn(turn)


def loose_path(block, rank, pair_low, row_points, couple, point_factor):
    fourier = block.reshape(BANDS, 2, 2, 2, 2, 64)[..., :ROWS]
    fourier = jnp.transpose(fourier, (0, 1, 2, 4, 3, 5)).reshape(64, 2, 2, ROWS).astype(F32)
    wave_list = jnp.stack([pair_low, NMAX - pair_low], axis=1).reshape(-1)
    points = lax.dynamic_slice_in_dim(row_points, rank[0] * ROWS, ROWS)
    width = (points + NSECT - 1) // NSECT
    columns = jnp.arange(SECW, dtype=jnp.int32)
    cos_inner, sin_inner = cos_sin(wave_list[None, None, :] * columns[None, :, None], points)
    trig = jnp.concatenate([cos_inner, -sin_inner], axis=2).astype(BF16)
    start = jnp.arange(NSECT, dtype=jnp.int32)[None, :] * width[:, None]
    cos_outer, sin_outer = cos_sin(wave_list[None, None, :] * start[:, :, None], points)
    valid = (columns < width[:, None, None]) & (start[:, :, None] + columns < points[:, None, None])
    keep = 2 * wave_list[None, :] < points[:, None]
    fourier = jnp.where(jnp.transpose(keep)[:, None, None], fourier, 0.0)
    real = jnp.transpose(fourier[:, :, 0], (2, 1, 0))[:, :, None]
    imag = jnp.transpose(fourier[:, :, 1], (2, 1, 0))[:, :, None]
    cos_wide, sin_wide = cos_outer[:, None], sin_outer[:, None]
    rotated = SCALE * jnp.concatenate(
        [real * cos_wide - imag * sin_wide, real * sin_wide + imag * cos_wide], axis=3
    )
    tile = jnp.einsum("rhnq,rcq->rhnc", rotated.astype(BF16), trig, preferred_element_type=F32)
    tile = jnp.where(valid[:, None], tile, 0.0).astype(BF16)
    local = jnp.transpose(tile, (2, 1, 0, 3)).reshape(NSECT, 2, ROWS * SECW)
    grid = lax.all_to_all(local, "sect", split_axis=0, concat_axis=0, tiled=True)
    coupled = jnp.einsum("fhx,fg->ghx", grid, couple, preferred_element_type=F32)
    tendency = (coupled * point_factor[None, :, 0]).astype(BF16)
    received = lax.all_to_all(tendency, "sect", split_axis=0, concat_axis=0, tiled=True)
    rows = received.reshape(NSECT, 2, ROWS, SECW)
    sums = jnp.einsum("nhrc,rcq->rhnq", rows, trig, preferred_element_type=F32)
    cos_part, sin_part = sums[..., :64], sums[..., 64:]
    real_sum = jnp.sum(cos_wide * cos_part + sin_wide * sin_part, axis=2)
    imag_sum = jnp.sum(cos_wide * sin_part - sin_wide * cos_part, axis=2)
    summed = jnp.stack([real_sum, imag_sum], axis=3)
    scale = jnp.where(keep, 2.0 / (SCALE * points.astype(F32))[:, None], 0.0)
    analysis = (summed * scale[:, None, :, None]).astype(BF16)
    analysis = jnp.pad(analysis, ((0, 64 - ROWS), (0, 0), (0, 0), (0, 0)))
    analysis = jnp.transpose(analysis, (2, 3, 1, 0)).reshape(BANDS, 8, LANES)
    return jnp.transpose(grid, (1, 0, 2)), analysis


def rows_fit(row_points):
    width = ((row_points + NSECT - 1) // NSECT).reshape(BANDS, ROWS)
    member = jnp.array([[row in rows for row in range(ROWS)] for rows in GROUP_ROWS])
    total = jnp.sum(jnp.where(member[None], width[:, None], 0), axis=2)
    return jnp.max(total) <= LANES


def per_device(spec_in, pair_low, row_points, legendre, gauss_weight, couple, point_factor):
    rank = lax.axis_index(WAVE).astype(jnp.int32).reshape(1)
    outgoing = to_bands(pair_low, spec_in[:, :, 0], legendre)
    block = lax.all_to_all(outgoing, WAVE, split_axis=0, concat_axis=0, tiled=True)
    coarse, fine, trig, slots, pf, scale = make_tables(pair_low, row_points, point_factor)

    def cross(x):
        x = x.reshape(NSECT, GROUPS, 2, LANES)
        return lax.all_to_all(x, "sect", split_axis=0, concat_axis=0, tiled=True).reshape(LINES, LANES)

    def packed_path(block):
        grid = cross(synthesize(block, coarse, fine, trig, slots, scale))
        received = cross(tend_of(grid, couple, pf))
        return expand(row_points, grid), analyse(received, coarse, fine, trig, slots, scale)

    def every_slot(block):
        return loose_path(block, rank, pair_low, row_points, couple, point_factor)

    grid_field, analysis = lax.cond(rows_fit(row_points), packed_path, every_slot, block)
    back = lax.all_to_all(analysis, WAVE, split_axis=0, concat_axis=0, tiled=True)
    spec_out = project(pair_low, back, gauss_weight, legendre)
    return grid_field[:, :, None, :], spec_out.reshape(2, 2, 1, NMAX)


def solution(mesh):
    split = Mesh(mesh.devices.reshape(8, 2, mesh.shape["sect"]), ("wave_0", "wave_1", "sect"))
    in_specs = (
        P(WAVE, None, "sect", None),
        P(),
        P(),
        P(WAVE, None, None),
        P(),
        P(),
        P(None, "sect", WAVE),
    )
    out_specs = (P(None, None, "sect", WAVE), P(WAVE, None, "sect", None))
    return jax.shard_map(
        per_device, mesh=split, in_specs=in_specs, out_specs=out_specs, check_vma=False
    )
```

```python
import functools
import math

import jax
import jax.numpy as jnp
from jax import lax
from jax.experimental import pallas as pl
from jax.experimental.pallas import tpu as pltpu
from jax.sharding import Mesh
from jax.sharding import PartitionSpec as P

WAVE = ("wave_0", "wave_1")
NMAX = 640
ROWS = 40
SECW = 41
NSECT = 64
BANDS = 16
LANES = 128
GROUP_ROWS = [
    [0, 7, 16, 22, 31, 34],
    [9, 12, 25, 26, 39],
    [2, 10, 15, 20, 29, 36],
    [11, 18, 19, 32, 33],
    [4, 6, 13, 24, 28, 37],
    [1, 8, 14, 23, 30, 35],
    [3, 5, 17, 21, 27, 38],
]
GROUPS = len(GROUP_ROWS)
MOST = max(len(rows) for rows in GROUP_ROWS)
SCALE = 2.0 / math.sqrt(40960.0)
F32 = jnp.float32
BF16 = jnp.bfloat16
SMEM = pltpu.SMEM
GRANT = 12 * 2**20
FULL_GRANT = 60 * 1024 * 2**10


def wave_rank():
    return lax.axis_index(WAVE).astype(jnp.int32)


def lane_iota(shape):
    return lax.broadcasted_iota(jnp.int32, shape, len(shape) - 1)


COS_TERMS = (6.52745434, -25.9667114, 60.1673855, -85.4501082, 64.9391157, -19.7392045, 0.999999989)
SIN_TERMS = (3.23767246, -14.8995044, 42.0258325, -76.7030033, 81.6051307, -41.3417004, 6.2831853)


def turn_part(product, points):
    inverse = 1.0 / points
    whole_turns = jnp.floor(product * inverse + 0.5)
    return (product - whole_turns * points) * inverse


def series(terms, square):
    value = terms[0] * square + terms[1]
    for term in terms[2:]:
        value = value * square + term
    return value


def cos_turn(turn):
    return series(COS_TERMS, turn * turn)


def sin_turn(turn):
    return turn * series(SIN_TERMS, turn * turn)


def wave_lanes(low_ref, shape):
    lane = lane_iota(shape)
    low = jnp.zeros(shape, jnp.int32)
    for pair in range(32):
        low = jnp.where((lane >> 2) == pair, low_ref[pair], low)
    return jnp.where(((lane >> 1) & 1) == 0, low, NMAX - low)


def group_offsets(points_ref, first, group):
    found = []
    offset = jnp.int32(0)
    for row in GROUP_ROWS[group]:
        points = points_ref[first + row]
        width = (points + (NSECT - 1)) >> 6
        found.append((row, points, width, offset))
        offset = offset + width
    return found


def tables_kernel(low_ref, points_ref, factor_ref, coarse_ref, fine_ref, trig_ref, slot_ref, pf_ref, scale_ref, pick_ref, pad_ref):
    rank = wave_rank()
    first = rank * ROWS
    for p in range(2):
        leading, odd = slot_signs(low_ref[2 * rank + p], (1, NMAX))
        pick_ref[p : p + 1, :] = jnp.where(leading, 0, 2) + jnp.where(odd, 4, 0)
    waves = wave_lanes(low_ref, (8, LANES))
    waves_f = waves.astype(F32)
    wave_row = waves_f[0:1]
    line = lax.broadcasted_iota(jnp.int32, (8, LANES), 0).astype(F32)
    odd_lane = (lane_iota((8, LANES)) & 1).astype(F32)
    fine_step = waves_f * line
    coarse_step = fine_step * 8.0
    back_quarter = odd_lane * 0.75
    scale_ref[...] = jnp.zeros((LANES, LANES), F32)
    for row in range(ROWS):
        length = jnp.full((8, LANES), points_ref[first + row], jnp.int32)
        points = length.astype(F32)
        width = ((length + (NSECT - 1)) >> 6).astype(F32)
        fine = turn_part(fine_step * width, points)
        fine_ref[0, row] = cos_turn(fine)
        fine_ref[1, row] = sin_turn(fine)
        coarse = turn_part(coarse_step * width + back_quarter * points, points)
        coarse_ref[0, row] = cos_turn(coarse)
        coarse_ref[1, row] = -sin_turn(coarse)
        keep = jnp.where(2 * waves < length, (2.0 / SCALE) / points, 0.0)[0:1]
        scale_ref[row : row + 1, :] = keep
        scale_ref[64 + row : 65 + row, :] = keep
    wave_col = jnp.transpose(jnp.broadcast_to(wave_row, (LANES, LANES)))
    quarter = (lax.broadcasted_iota(jnp.int32, (LANES, LANES), 0) & 1).astype(F32) * 0.25
    slot = lane_iota((1, LANES))
    for h in range(2):
        pad_ref[h : h + 1, 0 : ROWS * SECW] = factor_ref[h]
    for group in range(GROUPS):
        which = jnp.full((1, LANES), -1, jnp.int32)
        column = jnp.zeros((1, LANES), jnp.int32)
        points = jnp.full((1, LANES), 20, jnp.int32)
        width = jnp.zeros((1, LANES), jnp.int32)
        packed = jnp.zeros((8, LANES), F32)
        for i, (row, row_points, row_width, offset) in enumerate(group_offsets(points_ref, first, group)):
            mine = (slot >= offset) & (slot < offset + row_width)
            which = jnp.where(mine, i, which)
            column = jnp.where(mine, slot - offset, column)
            points = jnp.where(mine, row_points, points)
            width = jnp.where(mine, row_width, width)
            start = row * SECW
            base, shift = (start // LANES) * LANES, start % LANES
            window = pltpu.roll(pad_ref[:, base : base + 2 * LANES], 2 * LANES - shift, axis=1)[:, 0:LANES]
            packed = jnp.where(mine, pltpu.roll(window, offset & (LANES - 1), axis=1), packed)
        slot_ref[0, group : group + 1, :] = which
        slot_ref[1, group : group + 1, :] = width
        slot_ref[2, group : group + 1, :] = points - column
        for h in range(2):
            pf_ref[h, group : group + 1, :] = packed[h : h + 1]
        points = jnp.broadcast_to(points.astype(F32), (LANES, LANES))
        turn = turn_part(wave_col * column.astype(F32) + quarter * points, points)
        trig_ref[group] = cos_turn(turn).astype(BF16)


def synth_kernel(block_ref, coarse_ref, fine_ref, trig_ref, slot_ref, scale_ref, out_ref, a_ref, b_ref, lhs_ref, row_ref):
    even = (lane_iota((LANES, LANES)) & 1) == 0
    coeffs = jnp.transpose(block_ref[...].reshape(LANES, LANES).astype(F32))
    coeffs = jnp.where(scale_ref[...] > 0.0, coeffs, 0.0) * SCALE
    a_ref[...] = jnp.where(even, coeffs, pltpu.roll(coeffs, 1, axis=1))
    b_ref[...] = jnp.where(even, pltpu.roll(coeffs, LANES - 1, axis=1), coeffs)
    sector = lax.broadcasted_iota(jnp.int32, (NSECT, LANES), 0)
    for group in range(GROUPS):
        used = 2 * NSECT * len(GROUP_ROWS[group])
        for i, row in enumerate(GROUP_ROWS[group]):
            cos = fine_ref[0, row]
            sin = fine_ref[1, row]
            for h in range(2):
                at = h * 64 + row
                a = a_ref[at : at + 1, :]
                b = b_ref[at : at + 1, :]
                near = a * cos - b * sin
                far = a * sin + b * cos
                for block in range(0, 8, 2):
                    pair = [
                        coarse_ref[0, row, k : k + 1, :] * near + coarse_ref[1, row, k : k + 1, :] * far
                        for k in (block, block + 1)
                    ]
                    place = (i * 2 + h) * NSECT + block * 8
                    lhs_ref[place : place + 16, :] = jnp.concatenate(pair, axis=0).astype(BF16)
        product = jnp.dot(lhs_ref[0:used, :], trig_ref[group], preferred_element_type=F32)
        which = slot_ref[0, group : group + 1, :]
        valid = sector * slot_ref[1, group : group + 1, :] < slot_ref[2, group : group + 1, :]
        which = jnp.where(valid, which, -1)
        for h in range(2):
            total = jnp.zeros((NSECT, LANES), F32)
            for i in range(len(GROUP_ROWS[group])):
                place = (i * 2 + h) * NSECT
                total = jnp.where(which == i, product[place : place + NSECT, :], total)
            row_ref[pl.ds(2 * group + h, NSECT, stride=2 * GROUPS), :] = total
    out_ref[...] = row_ref[...].astype(BF16)


def rows_of(ref):
    return ref[...].astype(F32)


def tendency_kernel(grid_ref, couple_ref, pf_ref, out_ref, row_ref):
    row_ref[...] = rows_of(grid_ref)
    couple = jnp.transpose(couple_ref[...].astype(F32)).astype(BF16)
    tends = []
    for line in range(2 * GROUPS):
        values = row_ref[pl.ds(line, NSECT, stride=2 * GROUPS), :].astype(BF16)
        coupled = jnp.dot(couple, values, preferred_element_type=F32)
        group, h = divmod(line, 2)
        tends.append(coupled * pf_ref[h, group : group + 1, :])
    for line in range(2 * GROUPS):
        row_ref[pl.ds(line, NSECT, stride=2 * GROUPS), :] = tends[line]
    out_ref[...] = row_ref[...].astype(BF16)


def expand_kernel(points_ref, grid_ref, out_ref, row_ref, wide_ref):
    first = wave_rank() * ROWS
    row_ref[...] = rows_of(grid_ref)
    lane = lane_iota((NSECT, LANES))
    tiles = -(-ROWS * SECW // LANES)
    info = {}
    for group in range(GROUPS):
        for row, _, width, offset in group_offsets(points_ref, first, group):
            info[row] = (group, width, offset)
    for h in range(2):
        for tile in range(tiles):
            total = jnp.zeros((NSECT, LANES), F32)
            for row in range(ROWS):
                start = row * SECW - tile * LANES
                if start >= LANES or start + SECW <= 0:
                    continue
                group, width, offset = info[row]
                values = row_ref[pl.ds(2 * group + h, NSECT, stride=2 * GROUPS), :]
                values = pltpu.roll(values, (start + 2 * LANES - offset) & (LANES - 1), axis=1)
                total = jnp.where((lane >= start) & (lane < start + width), values, total)
            wide_ref[:, tile * LANES : (tile + 1) * LANES] = total
        out_ref[h] = wide_ref[:, 0 : ROWS * SECW].astype(BF16)


def analysis_kernel(tend_ref, coarse_ref, fine_ref, trig_ref, slot_ref, scale_ref, out_ref, row_ref, lhs_ref, yu_ref, yw_ref):
    row_ref[...] = rows_of(tend_ref)
    yu_ref[...] = jnp.zeros((LANES, LANES), F32)
    yw_ref[...] = jnp.zeros((LANES, LANES), F32)
    for group in range(GROUPS):
        which = slot_ref[0, group : group + 1, :]
        used = 2 * NSECT * len(GROUP_ROWS[group])
        for h in range(2):
            values = row_ref[pl.ds(2 * group + h, NSECT, stride=2 * GROUPS), :]
            for i in range(len(GROUP_ROWS[group])):
                place = (i * 2 + h) * NSECT
                lhs_ref[place : place + NSECT, :] = jnp.where(which == i, values, 0.0).astype(BF16)
        product = lax.dot_general(
            lhs_ref[0:used, :], trig_ref[group], (((1,), (1,)), ((), ())), preferred_element_type=F32
        )
        for i, row in enumerate(GROUP_ROWS[group]):
            cos = fine_ref[0, row]
            sin = fine_ref[1, row]
            for h in range(2):
                near = jnp.zeros((8, LANES), F32)
                far = jnp.zeros((8, LANES), F32)
                for block in range(8):
                    place = (i * 2 + h) * NSECT + block * 8
                    sums = product[place : place + 8, :]
                    near = near + sums * coarse_ref[0, row, block : block + 1, :]
                    far = far + sums * coarse_ref[1, row, block : block + 1, :]
                at = h * 64 + row
                yu_ref[at : at + 1, :] = jnp.sum(near * cos + far * sin, axis=0, keepdims=True)
                yw_ref[at : at + 1, :] = jnp.sum(far * cos - near * sin, axis=0, keepdims=True)
    even = (lane_iota((LANES, LANES)) & 1) == 0
    yu = yu_ref[...]
    yw = yw_ref[...]
    real = yu + pltpu.roll(yu, LANES - 1, axis=1)
    imag = yw + pltpu.roll(yw, 1, axis=1)
    result = jnp.where(even, real, imag) * scale_ref[...]
    out_ref[...] = jnp.transpose(result).astype(BF16).reshape(BANDS, 8, LANES)


def slot_signs(low, shape):
    slot = lane_iota(shape)
    leading = slot < NMAX - low
    odd = jnp.where(leading, slot & 1, (slot + low) & 1) == 1
    return leading, odd


def legendre_kernel(low_hbm, spec_hbm, leg_hbm, out_ref, wide_ref, low_ref, spec_ref, leg_ref, sems):
    low_copy = pltpu.make_async_copy(low_hbm, low_ref, sems.at[5])
    low_copy.start()
    spec_copy = pltpu.make_async_copy(spec_hbm, spec_ref, sems.at[4])
    spec_copy.start()
    half = NMAX // 2
    leg_copies = []
    for p in range(2):
        for part in range(2):
            rows = pl.ds(part * half, half)
            leg_copies.append(
                pltpu.make_async_copy(leg_hbm.at[p, rows], leg_ref.at[p, rows], sems.at[2 * p + part])
            )
            leg_copies[-1].start()
    wide_ref[...] = jnp.zeros((16, 6 * LANES), F32)
    line = lax.broadcasted_iota(jnp.int32, (8, NMAX), 0)
    h = line >> 2
    member = (line >> 1) & 1
    part = line & 1
    spec_copy.wait()
    low_copy.wait()
    values = []
    for p in range(2):
        low = low_ref[2 * wave_rank() + p]
        leading, odd = slot_signs(low, (8, NMAX))
        spec = spec_ref[p].astype(F32)
        value = jnp.where(part == 0, spec[0:1], spec[1:2])
        value = jnp.where((member == 0) == leading, value, 0.0)
        values.append(jnp.where((h == 1) & odd, -value, value).astype(BF16))
    found = []
    for p in range(2):
        leg_copies[2 * p].wait()
        leg_copies[2 * p + 1].wait()
        found.append(jnp.dot(values[p], leg_ref[p], preferred_element_type=F32))
    upper = line < 4
    wide_ref[0:8, 0:NMAX] = jnp.where(upper, found[0], pltpu.roll(found[1], 4, axis=0))
    wide_ref[8:16, 0:NMAX] = jnp.where(upper, pltpu.roll(found[0], 4, axis=0), found[1])
    lane = lane_iota((8, LANES))
    for band in range(BANDS):
        start = band * ROWS
        base, shift = (start // LANES) * LANES, start % LANES
        window = wide_ref[:, base : base + 2 * LANES]
        north = pltpu.roll(window[0:8], (2 * LANES - shift) % (2 * LANES), axis=1)[:, 0:LANES]
        south = pltpu.roll(window[8:16], (2 * LANES + 64 - shift) % (2 * LANES), axis=1)[:, 0:LANES]
        out_ref[band] = jnp.where(lane < 64, north, south).astype(BF16)


def project_kernel(pick_ref, back_ref, gauss_ref, leg_ref, out_ref, wide_ref):
    lane = lane_iota((8, LANES))
    for tile in range(NMAX // LANES):
        north = jnp.zeros((8, LANES), F32)
        south = jnp.zeros((8, LANES), F32)
        for band in range(BANDS):
            start = band * ROWS - tile * LANES
            if start >= LANES or start + ROWS <= 0:
                continue
            block = back_ref[band].astype(F32)
            mine = (lane >= start) & (lane < start + ROWS)
            north = jnp.where(mine, pltpu.roll(block, start % LANES, axis=1), north)
            south = jnp.where(mine, pltpu.roll(block, (start + 64) % LANES, axis=1), south)
        wide_ref[0:8, tile * LANES : (tile + 1) * LANES] = north
        wide_ref[8:16, tile * LANES : (tile + 1) * LANES] = south
    north = wide_ref[0:8, :]
    south = wide_ref[8:16, :]
    gauss = gauss_ref[...]
    both = (north + south) * gauss
    less = (north - south) * gauss
    upper = lax.broadcasted_iota(jnp.int32, (8, NMAX), 0) < 4
    forms = [
        jnp.where(upper, both, pltpu.roll(less, 4, axis=0)),
        jnp.where(upper, pltpu.roll(both, 4, axis=0), less),
    ]
    for p in range(2):
        pick = pick_ref[p : p + 1, :]
        product = lax.dot_general(
            forms[p].astype(BF16), leg_ref[p], (((1,), (1,)), ((), ())), preferred_element_type=F32
        )
        for r in range(2):
            chosen = product[r : r + 1]
            for first in (2, 4, 6):
                chosen = jnp.where(pick == first, product[first + r : first + r + 1], chosen)
            out_ref[2 * p + r] = chosen


def whole():
    return pl.BlockSpec(memory_space=pltpu.VMEM)


def in_hbm():
    return pl.BlockSpec(memory_space=pltpu.HBM)


def scalars():
    return pl.BlockSpec(memory_space=SMEM)


def run(kernel, name, outs, in_specs, scratch, *args, grant=GRANT):
    many = isinstance(outs, (list, tuple))
    return pl.pallas_call(
        kernel,
        out_shape=outs,
        in_specs=in_specs,
        out_specs=[whole() for _ in outs] if many else whole(),
        scratch_shapes=scratch,
        compiler_params=pltpu.CompilerParams(vmem_limit_bytes=grant),
        name=name,
    )(*args)


def struct(shape, dtype):
    return jax.ShapeDtypeStruct(shape, dtype)


def vmem(shape, dtype):
    return pltpu.VMEM(shape, dtype)


def make_tables(pair_low, row_points, point_factor):
    return run(
        tables_kernel,
        "tables",
        [
            struct((2, ROWS, 8, LANES), F32),
            struct((2, ROWS, 8, LANES), F32),
            struct((GROUPS, LANES, LANES), BF16),
            struct((3, GROUPS, LANES), jnp.int32),
            struct((2, GROUPS, LANES), F32),
            struct((LANES, LANES), F32),
            struct((2, NMAX), jnp.int32),
        ],
        [scalars(), scalars(), whole()],
        [vmem((8, 14 * LANES), F32)],
        pair_low, row_points, point_factor,
    )


LINES = NSECT * 2 * GROUPS


def synthesize(block, coarse, fine, trig, slots, scale):
    return run(
        synth_kernel,
        "synth",
        struct((LINES, LANES), BF16),
        [whole()] * 6,
        [
            vmem((LANES, LANES), F32),
            vmem((LANES, LANES), F32),
            vmem((2 * MOST * NSECT, LANES), BF16),
            vmem((LINES, LANES), F32),
        ],
        block, coarse, fine, trig, slots, scale,
    )


def tend_of(grid, couple, pf):
    return run(
        tendency_kernel,
        "tendency",
        struct((LINES, LANES), BF16),
        [whole()] * 3,
        [vmem((LINES, LANES), F32)],
        grid, couple, pf,
    )


def expand(row_points, grid):
    return run(
        expand_kernel,
        "expand",
        struct((2, NSECT, ROWS * SECW), BF16),
        [scalars(), whole()],
        [vmem((LINES, LANES), F32), vmem((NSECT, 13 * LANES), F32)],
        row_points, grid,
    )


def analyse(tend, coarse, fine, trig, slots, scale):
    return run(
        analysis_kernel,
        "analysis",
        struct((BANDS, 8, LANES), BF16),
        [whole()] * 6,
        [
            vmem((LINES, LANES), F32),
            vmem((2 * MOST * NSECT, LANES), BF16),
            vmem((LANES, LANES), F32),
            vmem((LANES, LANES), F32),
        ],
        tend, coarse, fine, trig, slots, scale,
    )


def to_bands(pair_low, spec, legendre):
    return run(
        legendre_kernel,
        "legendre",
        struct((BANDS, 8, LANES), BF16),
        [in_hbm(), in_hbm(), in_hbm()],
        [
            vmem((16, 6 * LANES), F32),
            SMEM((32,), jnp.int32),
            vmem((2, 2, NMAX), BF16),
            vmem((2, NMAX, NMAX), BF16),
            pltpu.SemaphoreType.DMA((6,)),
        ],
        pair_low, spec, legendre,
        grant=FULL_GRANT,
    )


def project(pick, back, gauss_weight, legendre):
    return run(
        project_kernel,
        "project",
        struct((4, 1, NMAX), F32),
        [whole()] * 4,
        [vmem((16, NMAX), F32)],
        pick, back, gauss_weight[None, :], legendre,
    )


def cos_sin(product, points):
    turn = turn_part(product.astype(F32), points.astype(F32)[:, None, None])
    return cos_turn(turn), sin_turn(turn)


def loose_path(block, rank, pair_low, row_points, couple, point_factor):
    fourier = block.reshape(BANDS, 2, 2, 2, 2, 64)[..., :ROWS]
    fourier = jnp.transpose(fourier, (0, 1, 2, 4, 3, 5)).reshape(64, 2, 2, ROWS).astype(F32)
    wave_list = jnp.stack([pair_low, NMAX - pair_low], axis=1).reshape(-1)
    points = lax.dynamic_slice_in_dim(row_points, rank[0] * ROWS, ROWS)
    width = (points + NSECT - 1) // NSECT
    columns = jnp.arange(SECW, dtype=jnp.int32)
    cos_inner, sin_inner = cos_sin(wave_list[None, None, :] * columns[None, :, None], points)
    trig = jnp.concatenate([cos_inner, -sin_inner], axis=2).astype(BF16)
    start = jnp.arange(NSECT, dtype=jnp.int32)[None, :] * width[:, None]
    cos_outer, sin_outer = cos_sin(wave_list[None, None, :] * start[:, :, None], points)
    valid = (columns < width[:, None, None]) & (start[:, :, None] + columns < points[:, None, None])
    keep = 2 * wave_list[None, :] < points[:, None]
    fourier = jnp.where(jnp.transpose(keep)[:, None, None], fourier, 0.0)
    real = jnp.transpose(fourier[:, :, 0], (2, 1, 0))[:, :, None]
    imag = jnp.transpose(fourier[:, :, 1], (2, 1, 0))[:, :, None]
    cos_wide, sin_wide = cos_outer[:, None], sin_outer[:, None]
    rotated = SCALE * jnp.concatenate(
        [real * cos_wide - imag * sin_wide, real * sin_wide + imag * cos_wide], axis=3
    )
    tile = jnp.einsum("rhnq,rcq->rhnc", rotated.astype(BF16), trig, preferred_element_type=F32)
    tile = jnp.where(valid[:, None], tile, 0.0).astype(BF16)
    local = jnp.transpose(tile, (2, 1, 0, 3)).reshape(NSECT, 2, ROWS * SECW)
    grid = lax.all_to_all(local, "sect", split_axis=0, concat_axis=0, tiled=True)
    coupled = jnp.einsum("fhx,fg->ghx", grid, couple, preferred_element_type=F32)
    tendency = (coupled * point_factor[None, :, 0]).astype(BF16)
    received = lax.all_to_all(tendency, "sect", split_axis=0, concat_axis=0, tiled=True)
    rows = received.reshape(NSECT, 2, ROWS, SECW)
    sums = jnp.einsum("nhrc,rcq->rhnq", rows, trig, preferred_element_type=F32)
    cos_part, sin_part = sums[..., :64], sums[..., 64:]
    real_sum = jnp.sum(cos_wide * cos_part + sin_wide * sin_part, axis=2)
    imag_sum = jnp.sum(cos_wide * sin_part - sin_wide * cos_part, axis=2)
    summed = jnp.stack([real_sum, imag_sum], axis=3)
    scale = jnp.where(keep, 2.0 / (SCALE * points.astype(F32))[:, None], 0.0)
    analysis = (summed * scale[:, None, :, None]).astype(BF16)
    analysis = jnp.pad(analysis, ((0, 64 - ROWS), (0, 0), (0, 0), (0, 0)))
    analysis = jnp.transpose(analysis, (2, 3, 1, 0)).reshape(BANDS, 8, LANES)
    return jnp.transpose(grid, (1, 0, 2)), analysis


def rows_fit(row_points):
    width = ((row_points + NSECT - 1) // NSECT).reshape(BANDS, ROWS)
    member = jnp.array([[row in rows for row in range(ROWS)] for rows in GROUP_ROWS])
    total = jnp.sum(jnp.where(member[None], width[:, None], 0), axis=2)
    return jnp.max(total) <= LANES


def per_device(spec_in, pair_low, row_points, legendre, gauss_weight, couple, point_factor):
    rank = lax.axis_index(WAVE).astype(jnp.int32).reshape(1)
    outgoing = to_bands(pair_low, spec_in[:, :, 0], legendre)
    block = lax.all_to_all(outgoing, WAVE, split_axis=0, concat_axis=0, tiled=True)
    coarse, fine, trig, slots, pf, scale, pick = make_tables(pair_low, row_points, point_factor)

    def cross(x):
        x = x.reshape(NSECT, GROUPS, 2, LANES)
        return lax.all_to_all(x, "sect", split_axis=0, concat_axis=0, tiled=True).reshape(LINES, LANES)

    def packed_path(block):
        grid = cross(synthesize(block, coarse, fine, trig, slots, scale))
        received = cross(tend_of(grid, couple, pf))
        return expand(row_points, grid), analyse(received, coarse, fine, trig, slots, scale)

    def every_slot(block):
        return loose_path(block, rank, pair_low, row_points, couple, point_factor)

    grid_field, analysis = lax.cond(rows_fit(row_points), packed_path, every_slot, block)
    back = lax.all_to_all(analysis, WAVE, split_axis=0, concat_axis=0, tiled=True)
    spec_out = project(pick, back, gauss_weight, legendre)
    return grid_field[:, :, None, :], spec_out.reshape(2, 2, 1, NMAX)


def solution(mesh):
    split = Mesh(mesh.devices.reshape(8, 2, mesh.shape["sect"]), ("wave_0", "wave_1", "sect"))
    in_specs = (
        P(WAVE, None, "sect", None),
        P(),
        P(),
        P(WAVE, None, None),
        P(),
        P(),
        P(None, "sect", WAVE),
    )
    out_specs = (P(None, None, "sect", WAVE), P(WAVE, None, "sect", None))
    return jax.shard_map(
        per_device, mesh=split, in_specs=in_specs, out_specs=out_specs, check_vma=False
    )
```

```python
import functools
import math

import jax
import jax.numpy as jnp
from jax import lax
from jax.experimental import pallas as pl
from jax.experimental.pallas import tpu as pltpu
from jax.sharding import Mesh
from jax.sharding import PartitionSpec as P

WAVE = ("wave_0", "wave_1")
NMAX = 640
ROWS = 40
SECW = 41
NSECT = 64
BANDS = 16
LANES = 128
GROUP_ROWS = [
    [0, 7, 16, 22, 31, 34],
    [9, 12, 25, 26, 39],
    [2, 10, 15, 20, 29, 36],
    [11, 18, 19, 32, 33],
    [4, 6, 13, 24, 28, 37],
    [1, 8, 14, 23, 30, 35],
    [3, 5, 17, 21, 27, 38],
]
GROUPS = len(GROUP_ROWS)
SCALE = 2.0 / math.sqrt(40960.0)
F32 = jnp.float32
BF16 = jnp.bfloat16
SMEM = pltpu.SMEM
GRANT = 12 * 2**20
PIECES = 5
FULL_GRANT = 60 * 1024 * 2**10


def wave_rank():
    return lax.axis_index(WAVE).astype(jnp.int32)


def lane_iota(shape):
    return lax.broadcasted_iota(jnp.int32, shape, len(shape) - 1)


COS_TERMS = (6.52745434, -25.9667114, 60.1673855, -85.4501082, 64.9391157, -19.7392045, 0.999999989)
SIN_TERMS = (3.23767246, -14.8995044, 42.0258325, -76.7030033, 81.6051307, -41.3417004, 6.2831853)


def turn_part(product, points):
    inverse = 1.0 / points
    whole_turns = jnp.floor(product * inverse + 0.5)
    return (product - whole_turns * points) * inverse


def series(terms, square):
    value = terms[0] * square + terms[1]
    for term in terms[2:]:
        value = value * square + term
    return value


def cos_turn(turn):
    return series(COS_TERMS, turn * turn)


def sin_turn(turn):
    return turn * series(SIN_TERMS, turn * turn)


def wave_lanes(low_ref, shape):
    lane = lane_iota(shape)
    low = jnp.zeros(shape, jnp.int32)
    for pair in range(32):
        low = jnp.where((lane >> 2) == pair, low_ref[pair], low)
    return jnp.where(((lane >> 1) & 1) == 0, low, NMAX - low)


def group_offsets(points_ref, first, group):
    found = []
    offset = jnp.int32(0)
    for row in GROUP_ROWS[group]:
        points = points_ref[first + row]
        width = (points + (NSECT - 1)) >> 6
        found.append((row, points, width, offset))
        offset = offset + width
    return found


def tables_kernel(low_ref, points_ref, factor_ref, coarse_ref, fine_ref, trig_ref, slot_ref, pf_ref, scale_ref, pick_ref, pad_ref):
    rank = wave_rank()
    first = rank * ROWS
    for p in range(2):
        leading, odd = slot_signs(low_ref[2 * rank + p], (1, NMAX))
        pick_ref[p : p + 1, :] = jnp.where(leading, 0, 2) + jnp.where(odd, 4, 0)
    waves = wave_lanes(low_ref, (8, LANES))
    waves_f = waves.astype(F32)
    wave_row = waves_f[0:1]
    line = lax.broadcasted_iota(jnp.int32, (8, LANES), 0).astype(F32)
    odd_lane = (lane_iota((8, LANES)) & 1).astype(F32)
    fine_step = waves_f * line
    coarse_step = fine_step * 8.0
    back_quarter = odd_lane * 0.75
    scale_ref[...] = jnp.zeros((LANES, LANES), F32)
    for row in range(ROWS):
        length = jnp.full((8, LANES), points_ref[first + row], jnp.int32)
        points = length.astype(F32)
        width = ((length + (NSECT - 1)) >> 6).astype(F32)
        fine = turn_part(fine_step * width, points)
        fine_ref[0, row] = cos_turn(fine)
        fine_ref[1, row] = sin_turn(fine)
        coarse = turn_part(coarse_step * width + back_quarter * points, points)
        coarse_ref[0, row] = cos_turn(coarse)
        coarse_ref[1, row] = -sin_turn(coarse)
        keep = jnp.where(2 * waves < length, (2.0 / SCALE) / points, 0.0)[0:1]
        scale_ref[row : row + 1, :] = keep
        scale_ref[64 + row : 65 + row, :] = keep
    wave_col = jnp.transpose(jnp.broadcast_to(wave_row, (LANES, LANES)))
    quarter = (lax.broadcasted_iota(jnp.int32, (LANES, LANES), 0) & 1).astype(F32) * 0.25
    slot = lane_iota((1, LANES))
    for h in range(2):
        pad_ref[h : h + 1, 0 : ROWS * SECW] = factor_ref[h]
    for group in range(GROUPS):
        which = jnp.full((1, LANES), -1, jnp.int32)
        column = jnp.zeros((1, LANES), jnp.int32)
        points = jnp.full((1, LANES), 20, jnp.int32)
        width = jnp.zeros((1, LANES), jnp.int32)
        packed = jnp.zeros((8, LANES), F32)
        for i, (row, row_points, row_width, offset) in enumerate(group_offsets(points_ref, first, group)):
            mine = (slot >= offset) & (slot < offset + row_width)
            which = jnp.where(mine, i, which)
            column = jnp.where(mine, slot - offset, column)
            points = jnp.where(mine, row_points, points)
            width = jnp.where(mine, row_width, width)
            start = row * SECW
            base, shift = (start // LANES) * LANES, start % LANES
            window = pltpu.roll(pad_ref[:, base : base + 2 * LANES], 2 * LANES - shift, axis=1)[:, 0:LANES]
            packed = jnp.where(mine, pltpu.roll(window, offset & (LANES - 1), axis=1), packed)
        slot_ref[0, group : group + 1, :] = which
        slot_ref[1, group : group + 1, :] = width
        slot_ref[2, group : group + 1, :] = jnp.where(which < 0, 0, points - column)
        for h in range(2):
            pf_ref[h, group : group + 1, :] = packed[h : h + 1]
        points = jnp.broadcast_to(points.astype(F32), (LANES, LANES))
        turn = turn_part(wave_col * column.astype(F32) + quarter * points, points)
        trig_ref[group] = cos_turn(turn).astype(BF16)


def synth_kernel(block_ref, coarse_ref, fine_ref, trig_ref, slot_ref, scale_ref, out_ref, a_ref, b_ref, row_ref):
    even = (lane_iota((LANES, LANES)) & 1) == 0
    coeffs = jnp.transpose(block_ref[...].reshape(LANES, LANES).astype(F32))
    coeffs = jnp.where(scale_ref[...] > 0.0, coeffs, 0.0) * SCALE
    a_ref[...] = jnp.where(even, coeffs, pltpu.roll(coeffs, 1, axis=1))
    b_ref[...] = jnp.where(even, pltpu.roll(coeffs, LANES - 1, axis=1), coeffs)
    sector = lax.broadcasted_iota(jnp.int32, (NSECT, LANES), 0)
    for group in range(GROUPS):
        which = slot_ref[0, group : group + 1, :]
        total = None
        for i, row in enumerate(GROUP_ROWS[group]):
            cos = fine_ref[0, row]
            sin = fine_ref[1, row]
            us = [coarse_ref[0, row, k : k + 1, :] for k in range(8)]
            ws = [coarse_ref[1, row, k : k + 1, :] for k in range(8)]
            tiles = []
            for h in range(2):
                at = h * 64 + row
                a = a_ref[at : at + 1, :]
                b = b_ref[at : at + 1, :]
                near = a * cos - b * sin
                far = a * sin + b * cos
                tiles += [us[k] * near + ws[k] * far for k in range(8)]
            lhs = jnp.concatenate(tiles, axis=0).astype(BF16)
            product = jnp.dot(lhs, trig_ref[group], preferred_element_type=F32)
            total = product if total is None else jnp.where(which == i, product, total)
        valid = sector * slot_ref[1, group : group + 1, :] < slot_ref[2, group : group + 1, :]
        for h in range(2):
            part = jnp.where(valid, total[h * NSECT : (h + 1) * NSECT, :], 0.0)
            row_ref[pl.ds(2 * group + h, NSECT, stride=2 * GROUPS), :] = part
    out_ref[...] = row_ref[...].astype(BF16)


def rows_of(ref):
    return ref[...].astype(F32)


def tendency_kernel(grid_ref, couple_ref, pf_ref, out_ref, row_ref):
    row_ref[...] = rows_of(grid_ref)
    couple = jnp.transpose(couple_ref[...].astype(F32)).astype(BF16)
    tends = []
    for line in range(2 * GROUPS):
        values = row_ref[pl.ds(line, NSECT, stride=2 * GROUPS), :].astype(BF16)
        coupled = jnp.dot(couple, values, preferred_element_type=F32)
        group, h = divmod(line, 2)
        tends.append(coupled * pf_ref[h, group : group + 1, :])
    for line in range(2 * GROUPS):
        row_ref[pl.ds(line, NSECT, stride=2 * GROUPS), :] = tends[line]
    out_ref[...] = row_ref[...].astype(BF16)


def expand_kernel(points_ref, grid_ref, out_ref, row_ref, wide_ref):
    first = wave_rank() * ROWS
    row_ref[...] = rows_of(grid_ref)
    lane = lane_iota((NSECT, LANES))
    tiles = -(-ROWS * SECW // LANES)
    info = {}
    for group in range(GROUPS):
        for row, _, width, offset in group_offsets(points_ref, first, group):
            info[row] = (group, width, offset)
    for h in range(2):
        for tile in range(tiles):
            total = jnp.zeros((NSECT, LANES), F32)
            for row in range(ROWS):
                start = row * SECW - tile * LANES
                if start >= LANES or start + SECW <= 0:
                    continue
                group, width, offset = info[row]
                values = row_ref[pl.ds(2 * group + h, NSECT, stride=2 * GROUPS), :]
                values = pltpu.roll(values, (start + 2 * LANES - offset) & (LANES - 1), axis=1)
                total = jnp.where((lane >= start) & (lane < start + width), values, total)
            wide_ref[:, tile * LANES : (tile + 1) * LANES] = total
        out_ref[h] = wide_ref[:, 0 : ROWS * SECW].astype(BF16)


def analysis_kernel(tend_ref, coarse_ref, fine_ref, trig_ref, slot_ref, scale_ref, out_ref, row_ref, yu_ref, yw_ref):
    row_ref[...] = rows_of(tend_ref)
    yu_ref[...] = jnp.zeros((LANES, LANES), F32)
    yw_ref[...] = jnp.zeros((LANES, LANES), F32)
    for group in range(GROUPS):
        which = slot_ref[0, group : group + 1, :]
        values = jnp.concatenate(
            [row_ref[pl.ds(2 * group + h, NSECT, stride=2 * GROUPS), :] for h in range(2)], axis=0
        )
        for i, row in enumerate(GROUP_ROWS[group]):
            lhs = jnp.where(which == i, values, 0.0).astype(BF16)
            product = lax.dot_general(
                lhs, trig_ref[group], (((1,), (1,)), ((), ())), preferred_element_type=F32
            )
            cos = fine_ref[0, row]
            sin = fine_ref[1, row]
            us = [coarse_ref[0, row, k : k + 1, :] for k in range(8)]
            ws = [coarse_ref[1, row, k : k + 1, :] for k in range(8)]
            for h in range(2):
                near = jnp.zeros((8, LANES), F32)
                far = jnp.zeros((8, LANES), F32)
                for k in range(8):
                    sums = product[h * NSECT + 8 * k : h * NSECT + 8 * k + 8, :]
                    near = near + sums * us[k]
                    far = far + sums * ws[k]
                at = h * 64 + row
                yu_ref[at : at + 1, :] = jnp.sum(near * cos + far * sin, axis=0, keepdims=True)
                yw_ref[at : at + 1, :] = jnp.sum(far * cos - near * sin, axis=0, keepdims=True)
    even = (lane_iota((LANES, LANES)) & 1) == 0
    yu = yu_ref[...]
    yw = yw_ref[...]
    real = yu + pltpu.roll(yu, LANES - 1, axis=1)
    imag = yw + pltpu.roll(yw, 1, axis=1)
    result = jnp.where(even, real, imag) * scale_ref[...]
    out_ref[...] = jnp.transpose(result).astype(BF16).reshape(BANDS, 8, LANES)


def slot_signs(low, shape):
    slot = lane_iota(shape)
    leading = slot < NMAX - low
    odd = jnp.where(leading, slot & 1, (slot + low) & 1) == 1
    return leading, odd


def legendre_kernel(low_hbm, spec_hbm, leg_hbm, out_ref, wide_ref, low_ref, spec_ref, leg_ref, sems):
    low_copy = pltpu.make_async_copy(low_hbm, low_ref, sems.at[2 * PIECES + 1])
    low_copy.start()
    spec_copy = pltpu.make_async_copy(spec_hbm, spec_ref, sems.at[2 * PIECES])
    spec_copy.start()
    piece = NMAX // PIECES
    leg_copies = []
    for p in range(2):
        for part in range(PIECES):
            rows = pl.ds(part * piece, piece)
            leg_copies.append(
                pltpu.make_async_copy(leg_hbm.at[p, rows], leg_ref.at[p, rows], sems.at[PIECES * p + part])
            )
            leg_copies[-1].start()
    wide_ref[...] = jnp.zeros((16, 6 * LANES), F32)
    line = lax.broadcasted_iota(jnp.int32, (8, NMAX), 0)
    h = line >> 2
    member = (line >> 1) & 1
    part = line & 1
    spec_copy.wait()
    low_copy.wait()
    values = []
    for p in range(2):
        low = low_ref[2 * wave_rank() + p]
        leading, odd = slot_signs(low, (8, NMAX))
        spec = spec_ref[p].astype(F32)
        value = jnp.where(part == 0, spec[0:1], spec[1:2])
        value = jnp.where((member == 0) == leading, value, 0.0)
        values.append(jnp.where((h == 1) & odd, -value, value).astype(BF16))
    found = []
    for p in range(2):
        for part in range(PIECES):
            leg_copies[PIECES * p + part].wait()
        found.append(jnp.dot(values[p], leg_ref[p], preferred_element_type=F32))
    upper = line < 4
    wide_ref[0:8, 0:NMAX] = jnp.where(upper, found[0], pltpu.roll(found[1], 4, axis=0))
    wide_ref[8:16, 0:NMAX] = jnp.where(upper, pltpu.roll(found[0], 4, axis=0), found[1])
    lane = lane_iota((8, LANES))
    for band in range(BANDS):
        start = band * ROWS
        base, shift = (start // LANES) * LANES, start % LANES
        window = wide_ref[:, base : base + 2 * LANES]
        north = pltpu.roll(window[0:8], (2 * LANES - shift) % (2 * LANES), axis=1)[:, 0:LANES]
        south = pltpu.roll(window[8:16], (2 * LANES + 64 - shift) % (2 * LANES), axis=1)[:, 0:LANES]
        out_ref[band] = jnp.where(lane < 64, north, south).astype(BF16)


def project_kernel(pick_ref, back_ref, gauss_ref, leg_ref, out_ref, wide_ref):
    lane = lane_iota((8, LANES))
    for tile in range(NMAX // LANES):
        north = jnp.zeros((8, LANES), F32)
        south = jnp.zeros((8, LANES), F32)
        for band in range(BANDS):
            start = band * ROWS - tile * LANES
            if start >= LANES or start + ROWS <= 0:
                continue
            block = back_ref[band].astype(F32)
            mine = (lane >= start) & (lane < start + ROWS)
            north = jnp.where(mine, pltpu.roll(block, start % LANES, axis=1), north)
            south = jnp.where(mine, pltpu.roll(block, (start + 64) % LANES, axis=1), south)
        wide_ref[0:8, tile * LANES : (tile + 1) * LANES] = north
        wide_ref[8:16, tile * LANES : (tile + 1) * LANES] = south
    north = wide_ref[0:8, :]
    south = wide_ref[8:16, :]
    gauss = gauss_ref[...]
    both = (north + south) * gauss
    less = (north - south) * gauss
    upper = lax.broadcasted_iota(jnp.int32, (8, NMAX), 0) < 4
    forms = [
        jnp.where(upper, both, pltpu.roll(less, 4, axis=0)),
        jnp.where(upper, pltpu.roll(both, 4, axis=0), less),
    ]
    for p in range(2):
        pick = pick_ref[p : p + 1, :]
        product = lax.dot_general(
            forms[p].astype(BF16), leg_ref[p], (((1,), (1,)), ((), ())), preferred_element_type=F32
        )
        for r in range(2):
            chosen = product[r : r + 1]
            for first in (2, 4, 6):
                chosen = jnp.where(pick == first, product[first + r : first + r + 1], chosen)
            out_ref[2 * p + r] = chosen


def whole():
    return pl.BlockSpec(memory_space=pltpu.VMEM)


def in_hbm():
    return pl.BlockSpec(memory_space=pltpu.HBM)


def scalars():
    return pl.BlockSpec(memory_space=SMEM)


def run(kernel, name, outs, in_specs, scratch, *args, grant=GRANT):
    many = isinstance(outs, (list, tuple))
    return pl.pallas_call(
        kernel,
        out_shape=outs,
        in_specs=in_specs,
        out_specs=[whole() for _ in outs] if many else whole(),
        scratch_shapes=scratch,
        compiler_params=pltpu.CompilerParams(vmem_limit_bytes=grant),
        name=name,
    )(*args)


def struct(shape, dtype):
    return jax.ShapeDtypeStruct(shape, dtype)


def vmem(shape, dtype):
    return pltpu.VMEM(shape, dtype)


def make_tables(pair_low, row_points, point_factor):
    return run(
        tables_kernel,
        "tables",
        [
            struct((2, ROWS, 8, LANES), F32),
            struct((2, ROWS, 8, LANES), F32),
            struct((GROUPS, LANES, LANES), BF16),
            struct((3, GROUPS, LANES), jnp.int32),
            struct((2, GROUPS, LANES), F32),
            struct((LANES, LANES), F32),
            struct((2, NMAX), jnp.int32),
        ],
        [scalars(), scalars(), whole()],
        [vmem((8, 14 * LANES), F32)],
        pair_low, row_points, point_factor,
    )


LINES = NSECT * 2 * GROUPS


def synthesize(block, coarse, fine, trig, slots, scale):
    return run(
        synth_kernel,
        "synth",
        struct((LINES, LANES), BF16),
        [whole()] * 6,
        [
            vmem((LANES, LANES), F32),
            vmem((LANES, LANES), F32),
            vmem((LINES, LANES), F32),
        ],
        block, coarse, fine, trig, slots, scale,
    )


def tend_of(grid, couple, pf):
    return run(
        tendency_kernel,
        "tendency",
        struct((LINES, LANES), BF16),
        [whole()] * 3,
        [vmem((LINES, LANES), F32)],
        grid, couple, pf,
    )


def expand(row_points, grid):
    return run(
        expand_kernel,
        "expand",
        struct((2, NSECT, ROWS * SECW), BF16),
        [scalars(), whole()],
        [vmem((LINES, LANES), F32), vmem((NSECT, 13 * LANES), F32)],
        row_points, grid,
    )


def analyse(tend, coarse, fine, trig, slots, scale):
    return run(
        analysis_kernel,
        "analysis",
        struct((BANDS, 8, LANES), BF16),
        [whole()] * 6,
        [
            vmem((LINES, LANES), F32),
            vmem((LANES, LANES), F32),
            vmem((LANES, LANES), F32),
        ],
        tend, coarse, fine, trig, slots, scale,
    )


def to_bands(pair_low, spec, legendre):
    return run(
        legendre_kernel,
        "legendre",
        struct((BANDS, 8, LANES), BF16),
        [in_hbm(), in_hbm(), in_hbm()],
        [
            vmem((16, 6 * LANES), F32),
            SMEM((32,), jnp.int32),
            vmem((2, 2, NMAX), BF16),
            vmem((2, NMAX, NMAX), BF16),
            pltpu.SemaphoreType.DMA((2 * PIECES + 2,)),
        ],
        pair_low, spec, legendre,
        grant=FULL_GRANT,
    )


def project(pick, back, gauss_weight, legendre):
    return run(
        project_kernel,
        "project",
        struct((4, 1, NMAX), F32),
        [whole()] * 4,
        [vmem((16, NMAX), F32)],
        pick, back, gauss_weight[None, :], legendre,
    )


def cos_sin(product, points):
    turn = turn_part(product.astype(F32), points.astype(F32)[:, None, None])
    return cos_turn(turn), sin_turn(turn)


def loose_path(block, rank, pair_low, row_points, couple, point_factor):
    fourier = block.reshape(BANDS, 2, 2, 2, 2, 64)[..., :ROWS]
    fourier = jnp.transpose(fourier, (0, 1, 2, 4, 3, 5)).reshape(64, 2, 2, ROWS).astype(F32)
    wave_list = jnp.stack([pair_low, NMAX - pair_low], axis=1).reshape(-1)
    points = lax.dynamic_slice_in_dim(row_points, rank[0] * ROWS, ROWS)
    width = (points + NSECT - 1) // NSECT
    columns = jnp.arange(SECW, dtype=jnp.int32)
    cos_inner, sin_inner = cos_sin(wave_list[None, None, :] * columns[None, :, None], points)
    trig = jnp.concatenate([cos_inner, -sin_inner], axis=2).astype(BF16)
    start = jnp.arange(NSECT, dtype=jnp.int32)[None, :] * width[:, None]
    cos_outer, sin_outer = cos_sin(wave_list[None, None, :] * start[:, :, None], points)
    valid = (columns < width[:, None, None]) & (start[:, :, None] + columns < points[:, None, None])
    keep = 2 * wave_list[None, :] < points[:, None]
    fourier = jnp.where(jnp.transpose(keep)[:, None, None], fourier, 0.0)
    real = jnp.transpose(fourier[:, :, 0], (2, 1, 0))[:, :, None]
    imag = jnp.transpose(fourier[:, :, 1], (2, 1, 0))[:, :, None]
    cos_wide, sin_wide = cos_outer[:, None], sin_outer[:, None]
    rotated = SCALE * jnp.concatenate(
        [real * cos_wide - imag * sin_wide, real * sin_wide + imag * cos_wide], axis=3
    )
    tile = jnp.einsum("rhnq,rcq->rhnc", rotated.astype(BF16), trig, preferred_element_type=F32)
    tile = jnp.where(valid[:, None], tile, 0.0).astype(BF16)
    local = jnp.transpose(tile, (2, 1, 0, 3)).reshape(NSECT, 2, ROWS * SECW)
    grid = lax.all_to_all(local, "sect", split_axis=0, concat_axis=0, tiled=True)
    coupled = jnp.einsum("fhx,fg->ghx", grid, couple, preferred_element_type=F32)
    tendency = (coupled * point_factor[None, :, 0]).astype(BF16)
    received = lax.all_to_all(tendency, "sect", split_axis=0, concat_axis=0, tiled=True)
    rows = received.reshape(NSECT, 2, ROWS, SECW)
    sums = jnp.einsum("nhrc,rcq->rhnq", rows, trig, preferred_element_type=F32)
    cos_part, sin_part = sums[..., :64], sums[..., 64:]
    real_sum = jnp.sum(cos_wide * cos_part + sin_wide * sin_part, axis=2)
    imag_sum = jnp.sum(cos_wide * sin_part - sin_wide * cos_part, axis=2)
    summed = jnp.stack([real_sum, imag_sum], axis=3)
    scale = jnp.where(keep, 2.0 / (SCALE * points.astype(F32))[:, None], 0.0)
    analysis = (summed * scale[:, None, :, None]).astype(BF16)
    analysis = jnp.pad(analysis, ((0, 64 - ROWS), (0, 0), (0, 0), (0, 0)))
    analysis = jnp.transpose(analysis, (2, 3, 1, 0)).reshape(BANDS, 8, LANES)
    return jnp.transpose(grid, (1, 0, 2)), analysis


def rows_fit(row_points):
    width = ((row_points + NSECT - 1) // NSECT).reshape(BANDS, ROWS)
    member = jnp.array([[row in rows for row in range(ROWS)] for rows in GROUP_ROWS])
    total = jnp.sum(jnp.where(member[None], width[:, None], 0), axis=2)
    return jnp.max(total) <= LANES


def per_device(spec_in, pair_low, row_points, legendre, gauss_weight, couple, point_factor):
    rank = lax.axis_index(WAVE).astype(jnp.int32).reshape(1)
    outgoing = to_bands(pair_low, spec_in[:, :, 0], legendre)
    block = lax.all_to_all(outgoing, WAVE, split_axis=0, concat_axis=0, tiled=True)
    coarse, fine, trig, slots, pf, scale, pick = make_tables(pair_low, row_points, point_factor)

    def cross(x):
        x = x.reshape(NSECT, GROUPS, 2, LANES)
        return lax.all_to_all(x, "sect", split_axis=0, concat_axis=0, tiled=True).reshape(LINES, LANES)

    def packed_path(block):
        grid = cross(synthesize(block, coarse, fine, trig, slots, scale))
        received = cross(tend_of(grid, couple, pf))
        return expand(row_points, grid), analyse(received, coarse, fine, trig, slots, scale)

    def every_slot(block):
        return loose_path(block, rank, pair_low, row_points, couple, point_factor)

    grid_field, analysis = lax.cond(rows_fit(row_points), packed_path, every_slot, block)
    back = lax.all_to_all(analysis, WAVE, split_axis=0, concat_axis=0, tiled=True)
    spec_out = project(pick, back, gauss_weight, legendre)
    return grid_field[:, :, None, :], spec_out.reshape(2, 2, 1, NMAX)


def solution(mesh):
    split = Mesh(mesh.devices.reshape(8, 2, mesh.shape["sect"]), ("wave_0", "wave_1", "sect"))
    in_specs = (
        P(WAVE, None, "sect", None),
        P(),
        P(),
        P(WAVE, None, None),
        P(),
        P(),
        P(None, "sect", WAVE),
    )
    out_specs = (P(None, None, "sect", WAVE), P(WAVE, None, "sect", None))
    return jax.shard_map(
        per_device, mesh=split, in_specs=in_specs, out_specs=out_specs, check_vma=False
    )
```
